32 devices in a mesh: gx: 4 (over y, core), gy: 4 (over z), gz: 2 (over x).
Axes of the slice: x: 2, y: 2, z: 4, core: 2. Of those that a mesh axis runs over, the one named last changes fastest.
Arguments:
- field: float32 [64, 64, 16, 512], P(None, 'gz', 'gx', 'gy'), may hold values from 0.01 to 1
- courant_x: float32 [64, 16, 512], P('gz', 'gx', 'gy'), may hold values from -0.45 to 0.45
- courant_y: float32 [64, 16, 512], P('gz', 'gx', 'gy'), may hold values from -0.45 to 0.45
- supersat: float32 [64, 16, 512], P('gz', 'gx', 'gy'), may hold values from -0.5 to 0.5
- cloud_mask: int32 [64, 16, 512], P('gz', 'gx', 'gy'), may hold values 0 or 1
- fall_speed: float32 [64], replicated, may hold values from 0.05 to 40
- growth: float32 [47], replicated, may hold values from 0.2 to 1.6
- activation_threshold: float32 [16], replicated, may hold values from -0.2 to 0.4
- kernel_rate: float32 [48, 8], replicated, may hold values from 0.02 to 0.2
- partner: int32 [48, 8], replicated, may hold values from 0 to 47
- target: int32 [48, 8], replicated, may hold values from 0 to 47
Outputs:
- updated: float32 [64, 64, 16, 512], P(None, 'gz', 'gx', 'gy')
The draws below stay inside these ranges and needn't reach their ends.
Inputs may be any that keep to these rules, and one draw needn't show every extreme that they name: `partner`: bin indices of drop bins. `target`: bin indices of drop bins.
All inputs are finite; a program needn't handle non-finite values. No bound on the sum of `cloud_mask` on one device may be relied on, other than what follows from the above.
Results may differ from the reference program's by a relative error of at most 0.0003.
Values sent between devices are 32-bit elements; how exact they have to be, the bound alone decides.
A program may use at most 128 MiB of HBM per device.

```python
import math
import jax
import jax.numpy as jnp
from jax import lax

DROPS = 48
AERO = 16
BINS = 64
SLOTS = 8
NX = 16
NY = 512
NZ = 64


def set_ends(drawn, key, least, top_value):
    index_at = [jax.random.randint(jax.random.fold_in(key, axis), (), 0, length) for axis, length in enumerate(drawn.shape)]
    main_axis = drawn.shape.index(max(drawn.shape))
    neighbour = index_at[:main_axis] + [(index_at[main_axis] + 1) % drawn.shape[main_axis]] + index_at[main_axis + 1:]
    return drawn.at[tuple(index_at)].set(least).at[tuple(neighbour)].set(top_value)


def steps_of(own_key, shape, shards, least, high):
    def one(dim, blocks):
        steps = jax.random.uniform(jax.random.fold_in(jax.random.fold_in(own_key, 6), dim), (blocks,), jnp.float32, least / len(shards), high / len(shards))
        return jnp.repeat(jnp.exp(steps), shape[dim] // blocks).reshape((-1,) + (1,) * (len(shape) - dim - 1))

    loudness = one(*shards[0])
    for cut in shards[1:]:
        loudness = loudness * one(*cut)
    return loudness


def setup_inputs(seed: int = 0) -> dict:
    seeds = jax.random.split(jax.random.key(seed), 12)
    return {
        "field": jnp.clip(jnp.exp(math.log(1.0) - 4.6051702 * jax.random.uniform(seeds[0], (BINS, NZ, NX, NY), jnp.float32) ** steps_of(seeds[0], (BINS, NZ, NX, NY), ((1, 2), (2, 4), (3, 4)), -0.2, 0.2)), 0.01, 1.0),
        "courant_x": jnp.clip(jax.random.uniform(seeds[1], (NZ, NX, NY), jnp.float32, -0.45, 0.45) * steps_of(seeds[1], (NZ, NX, NY), ((0, 2), (1, 4), (2, 4)), -0.4, 0.0), -0.45, 0.45),
        "courant_y": jnp.clip(jax.random.uniform(seeds[2], (NZ, NX, NY), jnp.float32, -0.45, 0.45) * steps_of(seeds[2], (NZ, NX, NY), ((0, 2), (1, 4), (2, 4)), -0.4, 0.0), -0.45, 0.45),
        "supersat": jnp.clip(jax.random.uniform(seeds[3], (NZ, NX, NY), jnp.float32, -0.5, 0.5) * steps_of(seeds[3], (NZ, NX, NY), ((0, 2), (1, 4), (2, 4)), -0.4, 0.0), -0.5, 0.5),
        "cloud_mask": set_ends((jax.random.randint(seeds[4], (NZ, NX, NY), 0, 3) < 1).astype(jnp.int32), jax.random.fold_in(seeds[4], 1), 0, 1),
        "fall_speed": jnp.clip(jnp.exp(jax.random.uniform(seeds[5], (BINS,), jnp.float32, math.log(0.05), math.log(40.0))), 0.05, 40.0),
        "growth": jnp.clip(jnp.exp(jax.random.uniform(seeds[6], (DROPS - 1,), jnp.float32, math.log(0.2), math.log(1.6))), 0.2, 1.6),
        "activation_threshold": jnp.clip(jax.random.uniform(seeds[7], (AERO,), jnp.float32, -0.2, 0.4), -0.2, 0.4),
        "kernel_rate": jnp.clip(jnp.exp(jax.random.uniform(seeds[8], (DROPS, SLOTS), jnp.float32, math.log(0.02), math.log(0.2))), 0.02, 0.2),
        "partner": set_ends(jax.random.randint(seeds[9], (DROPS, SLOTS), 0, DROPS), jax.random.fold_in(seeds[9], 1), 0, DROPS - 1).astype(jnp.int32),
        "target": set_ends(jax.random.randint(seeds[10], (DROPS, SLOTS), 0, DROPS), jax.random.fold_in(seeds[10], 1), 0, DROPS - 1).astype(jnp.int32),
    }


def reference(field, courant_x, courant_y, supersat, cloud_mask, fall_speed, growth, activation_threshold, kernel_rate, partner, target):
    num_bins, num_levels, width_x, width_y = field.shape
    num_drops = growth.shape[0] + 1
    mask_float = cloud_mask.astype(jnp.float32)

    def one_row(index):
        left = jnp.mod(index - 1, width_x).astype(jnp.int32)
        right = jnp.mod(index + 1, width_x).astype(jnp.int32)
        q_left = lax.dynamic_index_in_dim(field, left, 2, keepdims=False)
        q_here = lax.dynamic_index_in_dim(field, index, 2, keepdims=False)
        q_right = lax.dynamic_index_in_dim(field, right, 2, keepdims=False)
        cour_here = lax.dynamic_index_in_dim(courant_x, index, 1, keepdims=False)
        cour_left = lax.dynamic_index_in_dim(courant_x, left, 1, keepdims=False)
        cour_y = lax.dynamic_index_in_dim(courant_y, index, 1, keepdims=False)
        sat_row = lax.dynamic_index_in_dim(supersat, index, 1, keepdims=False)
        mask_row = lax.dynamic_index_in_dim(mask_float, index, 1, keepdims=False)
        flux_right = jnp.maximum(cour_here, 0.0) * q_here + jnp.minimum(cour_here, 0.0) * q_right
        flux_left = jnp.maximum(cour_left, 0.0) * q_left + jnp.minimum(cour_left, 0.0) * q_here
        flux_up = jnp.maximum(cour_y, 0.0) * q_here + jnp.minimum(cour_y, 0.0) * jnp.roll(q_here, -1, axis=-1)
        flux_down = jnp.roll(flux_up, 1, axis=-1)
        advected = q_here - (flux_right - flux_left) - (flux_up - flux_down)

        def fall_step(carry, level):
            fresh = (level + fall_speed[:, None] * carry) / (1.0 + fall_speed[:, None])
            return fresh, fresh

        levels = jnp.moveaxis(advected, 1, 0)[::-1]
        _, fallen = lax.scan(fall_step, jnp.zeros((num_bins, width_y), jnp.float32), levels)
        settled = jnp.moveaxis(fallen[::-1], 0, 1)

        drop_mass = settled[:num_drops]
        aero_mass = settled[num_drops:]
        face = growth[:, None, None] * sat_row[None]
        cond_flux = jnp.maximum(face, 0.0) * drop_mass[:-1] + jnp.minimum(face, 0.0) * drop_mass[1:]
        zero_face = jnp.zeros_like(cond_flux[:1])
        grown = drop_mass + jnp.concatenate([zero_face, cond_flux], 0) - jnp.concatenate([cond_flux, zero_face], 0)
        activated = jnp.maximum(sat_row[None] - activation_threshold[:, None, None], 0.0) * aero_mass
        grown = jnp.concatenate([grown[:1] + jnp.sum(activated, 0, keepdims=True), grown[1:]], 0)
        aero_after = aero_mass - activated

        picked = grown[partner]
        rate = kernel_rate[:, :, None, None] * grown[:, None] * picked
        loss = jnp.sum(rate, 1)
        gain = jnp.zeros_like(grown).at[target.reshape(-1)].add(rate.reshape((-1,) + grown.shape[1:]))
        drops_after = grown + mask_row[None] * (gain - loss)
        return jnp.concatenate([drops_after, aero_after], 0)

    rows = lax.map(one_row, jnp.arange(width_x, dtype=jnp.int32))
    return jnp.transpose(rows, (1, 2, 0, 3))
```

```python
import functools

import jax
import jax.numpy as jnp
from jax import lax
from jax.experimental import pallas as pl
from jax.experimental.pallas import tpu as pltpu
from jax.sharding import PartitionSpec as P

LANES = 128
SUB = 8
GROUP = 8


def roll_to(value, source, dest):
    shift = (dest - source) % LANES
    return value if shift == 0 else pltpu.roll(value, shift, 1)


def pack_y_kernel(nx, field_ref, cour_ref, right_ref, left_ref):
    bins, rows, _ = field_ref.shape
    per_bin = rows // SUB
    blocks = rows // (SUB * nx)
    lane = lax.broadcasted_iota(jnp.int32, (SUB, LANES), 1)

    def one(load, offset, packed):
        for x in range(nx):
            for q in range(blocks):
                at = offset + x * blocks + q
                value = load(pl.ds(q * SUB * nx + x, SUB, stride=nx))
                hit = lane == at
                packed = (
                    jnp.where(hit, roll_to(value, LANES - 1, at), packed[0]),
                    jnp.where(hit, roll_to(value, 0, at), packed[1]),
                )
        return packed

    zero = jnp.zeros((SUB, LANES), jnp.float32)

    def group(g, _):
        packed = (zero, zero)
        for k in range(GROUP):
            packed = one(lambda r: field_ref[g * GROUP + k, r, :], k * per_bin, packed)
        right_ref[g] = packed[0]
        left_ref[g] = packed[1]
        return 0

    lax.fori_loop(0, bins // GROUP, group, 0)
    right_ref[bins // GROUP] = one(lambda r: cour_ref[r, :], 0, (zero, zero))[0]


def advect_settle_kernel(nx, xs, halos, *refs):
    if halos:
        scal, field, cx, cy, yl, yr, table, xl, xr, out, bottom = refs
    else:
        scal, field, cx, cy, yl, yr, table, out, bottom = refs
        xl = xr = None
    bins, rows, _ = field.shape
    blocks = rows // (SUB * nx)
    per_bin = nx * blocks
    lane = lax.broadcasted_iota(jnp.int32, (SUB, LANES), 1)
    first, last = lane == 0, lane == LANES - 1
    for xi, x in enumerate(xs):
        for q in reversed(range(blocks)):
            span = lambda xx: pl.ds(q * SUB * nx + xx, SUB, stride=nx)
            spot = x * blocks + q
            zrows = pl.ds(q * SUB, SUB)
            c_here = cx[span(x), :]
            c_left = cx[span(x - 1), :] if x > 0 else xl[bins, zrows, :]
            y_here = cy[span(x), :]
            y_left = jnp.where(
                first, roll_to(yl[bins // GROUP], spot, 0), pltpu.roll(y_here, 1, 1)
            )
            stay = (
                1.0
                - jnp.maximum(c_here, 0.0)
                + jnp.minimum(c_left, 0.0)
                - jnp.maximum(y_here, 0.0)
                + jnp.minimum(y_left, 0.0)
            )
            from_right = -jnp.minimum(c_here, 0.0)
            from_left = jnp.maximum(c_left, 0.0)
            from_up = -jnp.minimum(y_here, 0.0)
            from_down = jnp.maximum(y_left, 0.0)

            def group(g, _):
                down_pack = yl[g]
                up_pack = yr[g]
                for k in range(GROUP):
                    b = g * GROUP + k
                    here = field[b, span(x), :]
                    left = field[b, span(x - 1), :] if x > 0 else xl[b, zrows, :]
                    right = field[b, span(x + 1), :] if x < nx - 1 else xr[b, zrows, :]
                    at = k * per_bin + spot
                    down = jnp.where(first, roll_to(down_pack, at, 0), pltpu.roll(here, 1, 1))
                    up = jnp.where(
                        last, roll_to(up_pack, at, LANES - 1), pltpu.roll(here, LANES - 1, 1)
                    )
                    moved = (
                        stay * here
                        + from_right * right
                        + from_left * left
                        + from_up * up
                        + from_down * down
                    )
                    fall = moved * scal[b]
                    fall = fall + table[b, 0] * pltpu.roll(fall, SUB - 1, 0)
                    fall = fall + table[b, 1] * pltpu.roll(fall, SUB - 2, 0)
                    fall = fall + table[b, 2] * pltpu.roll(fall, SUB - 4, 0)
                    if q < blocks - 1:
                        above = out[b, xi * blocks + q + 1, pl.ds(0, 1), :]
                        fall = fall + table[b, 3] * above
                    out[b, xi * blocks + q] = fall
                    if q == 0:
                        bottom[xi, pl.ds(b, 1), :] = fall[0:1, :]
                return 0

            lax.fori_loop(0, bins // GROUP, group, 0)


def micro_kernel(nx, xs, slots, merge, *refs):
    if merge:
        scal, index, settled, carry, table, sat_ref, mask_ref, inner, out, grown, change = refs
    else:
        scal, index, settled, carry, table, sat_ref, mask_ref, out, grown, change = refs
    bins = settled.shape[0]
    drops = grown.shape[0]
    aero = bins - drops
    cells = grown.shape[1]
    blocks = cells // len(xs)
    at_growth = bins + blocks * bins
    at_threshold = at_growth + drops
    at_rate = at_threshold + aero

    def spans(v):
        x, q = xs[v // blocks], v % blocks
        return pl.ds(q * SUB * nx + x, SUB, stride=nx)

    sat = [sat_ref[spans(v), :] for v in range(cells)]

    def full(b):
        values = []
        decay = table[b, 3]
        for v in range(cells):
            xi, q = v // blocks, v % blocks
            values.append(
                settled[b, v]
                + (decay * scal[bins + q * bins + b]) * carry[xi, pl.ds(b, 1), :]
            )
        return values

    def put(b, v, value):
        if merge:
            out[b, spans(v), :] = value
        else:
            out[b, v] = value

    zero = jnp.zeros((SUB, LANES), jnp.float32)

    def activate(j, gained):
        mass = full(drops + j)
        fresh = []
        for v in range(cells):
            active = jnp.maximum(sat[v] - scal[at_threshold + j], 0.0) * mass[v]
            put(drops + j, v, mass[v] - active)
            fresh.append(gained[v] + active)
        return tuple(fresh)

    gained = lax.fori_loop(0, aero, activate, (zero,) * cells)

    def condense(b, state):
        current, below = state
        after = full(b + 1)
        flux = []
        for v in range(cells):
            face = scal[at_growth + b] * sat[v]
            flux.append(jnp.maximum(face, 0.0) * current[v] + jnp.minimum(face, 0.0) * after[v])
            grown[b, v] = current[v] + below[v] - flux[v]
            change[b, v] = zero
        return tuple(after), tuple(flux)

    current, below = lax.fori_loop(
        0, drops - 1, condense, (tuple(full(0)), (zero,) * cells)
    )
    for v in range(cells):
        grown[drops - 1, v] = current[v] + below[v]
        change[drops - 1, v] = zero
        grown[0, v] = grown[0, v] + gained[v]

    def collide(i, _):
        mine = grown[i]
        loss = jnp.zeros_like(mine)
        for m in range(slots):
            pair = i * slots + m
            rate = (mine * scal[at_rate + pair]) * grown[index[pair]]
            loss = loss + rate
            goal = index[drops * slots + pair]
            change[goal] = change[goal] + rate
        change[i] = change[i] - loss
        return 0

    lax.fori_loop(0, drops, collide, 0)

    mask = [mask_ref[spans(v), :].astype(jnp.float32) for v in range(cells)]

    def finish(b, _):
        for v in range(cells):
            put(b, v, grown[b, v] + mask[v] * change[b, v])
        return 0

    lax.fori_loop(0, drops, finish, 0)

    if merge:
        others = [x for x in range(nx) if x not in xs]

        def fill(b, _):
            for xi, x in enumerate(others):
                for q in range(blocks):
                    out[b, pl.ds(q * SUB * nx + x, SUB, stride=nx), :] = inner[b, xi * blocks + q]
            return 0

        lax.fori_loop(0, bins, fill, 0)


VMEM = pl.BlockSpec(memory_space=pltpu.VMEM)
SMEM = pl.BlockSpec(memory_space=pltpu.SMEM)
PARAMS = pltpu.CompilerParams(vmem_limit_bytes=48 * 1024 * 1024)


def cost(flops, bytes_accessed):
    return pl.CostEstimate(flops=flops, bytes_accessed=bytes_accessed, transcendentals=0)


def shift_up(value, axis):
    count = lax.axis_size(axis)
    return lax.ppermute(value, axis, [(i, (i + 1) % count) for i in range(count)])


def shift_down(value, axis):
    count = lax.axis_size(axis)
    return lax.ppermute(value, axis, [((i + 1) % count, i) for i in range(count)])


def shards(
    field,
    courant_x,
    courant_y,
    supersat,
    cloud_mask,
    fall_speed,
    growth,
    activation_threshold,
    kernel_rate,
    partner,
    target,
):
    bins, depth, nx, ny = field.shape
    drops, slots = partner.shape
    f32 = jnp.float32
    blocks = depth // SUB
    flat = field.reshape(bins, depth * nx, ny)
    cx, cy, sat, mask = (
        a.reshape(depth * nx, ny) for a in (courant_x, courant_y, supersat, cloud_mask)
    )

    to_right = jnp.concatenate([field[:, :, nx - 1, :], courant_x[None, :, nx - 1, :]], 0)
    to_left = field[:, :, 0, :]
    x_left = shift_up(to_right, "gx")
    x_right = shift_down(to_left, "gx")

    groups = bins // GROUP
    y_to_right, y_to_left = pl.pallas_call(
        functools.partial(pack_y_kernel, nx),
        out_shape=(
            jax.ShapeDtypeStruct((groups + 1, SUB, LANES), f32),
            jax.ShapeDtypeStruct((groups, SUB, LANES), f32),
        ),
        in_specs=[VMEM, VMEM],
        out_specs=(VMEM, VMEM),
        compiler_params=PARAMS,
        cost_estimate=cost(1 << 22, 1 << 22),
        name="pack_y",
    )(flat, cy)
    y_left = shift_up(y_to_right, "gy")
    y_right = shift_down(y_to_left, "gy")

    ratio = fall_speed / (1.0 + fall_speed)
    log_ratio = jnp.log(ratio)
    sub = jnp.arange(SUB, dtype=f32)
    power = jnp.stack([jnp.full((SUB,), 1.0, f32), jnp.full((SUB,), 2.0, f32), jnp.full((SUB,), 4.0, f32), SUB - sub])
    keep = jnp.stack([sub < SUB - 1, sub < SUB - 2, sub < SUB - 4, sub < SUB])
    table = jnp.where(keep, jnp.exp(log_ratio[:, None, None] * power), 0.0)
    table = jnp.broadcast_to(table[..., None], (bins, 4, SUB, LANES))
    step = jnp.exp(log_ratio[None, :] * (SUB * jnp.arange(blocks - 1, -1, -1, dtype=f32))[:, None])
    scal = jnp.concatenate(
        [
            1.0 / (1.0 + fall_speed),
            step.reshape(-1),
            growth,
            jnp.zeros((1,), f32),
            activation_threshold,
            kernel_rate.reshape(-1),
        ]
    )
    index = jnp.concatenate([partner.reshape(-1), target.reshape(-1)])

    inner_x = tuple(range(1, nx - 1))
    edge_x = (0, nx - 1)

    def settle_part(xs, halos):
        cells = len(xs) * blocks
        args = [scal, flat, cx, cy, y_left, y_right, table] + list(halos)
        return pl.pallas_call(
            functools.partial(advect_settle_kernel, nx, xs, bool(halos)),
            out_shape=(
                jax.ShapeDtypeStruct((bins, cells, SUB, LANES), f32),
                jax.ShapeDtypeStruct((len(xs), bins, LANES), f32),
            ),
            in_specs=[SMEM] + [VMEM] * (len(args) - 1),
            out_specs=(VMEM, VMEM),
            compiler_params=PARAMS,
            cost_estimate=cost(1 << 24, 8 << 20),
            name="settle_edge" if halos else "settle_inner",
        )(*args)

    count = lax.axis_size("gz")
    whole = jnp.exp(log_ratio * depth)[None, :, None]

    def inflow(bottom):
        carry = jnp.zeros_like(bottom)
        for hop in range(count - 1):
            sent = bottom if hop == 0 else bottom + whole * carry
            carry = lax.ppermute(sent, "gz", [(i + 1, i) for i in range(count - 1)])
        return carry

    def micro_part(xs, settled, carry, inner):
        cells = len(xs) * blocks
        args = [scal, index, settled, carry, table, sat, mask] + list(inner)
        if inner:
            out = jax.ShapeDtypeStruct((bins, depth * nx, ny), f32)
        else:
            out = jax.ShapeDtypeStruct((bins, cells, SUB, LANES), f32)
        return pl.pallas_call(
            functools.partial(micro_kernel, nx, xs, slots, bool(inner)),
            out_shape=out,
            in_specs=[SMEM, SMEM] + [VMEM] * (len(args) - 2),
            out_specs=VMEM,
            scratch_shapes=[
                pltpu.VMEM((drops, cells, SUB, LANES), f32),
                pltpu.VMEM((drops, cells, SUB, LANES), f32),
            ],
            compiler_params=PARAMS,
            cost_estimate=cost(1 << 24, 8 << 20),
            name="micro_edge" if inner else "micro_inner",
        )(*args)

    settled, bottom = settle_part(inner_x, ())
    inner = micro_part(inner_x, settled, inflow(bottom), ())
    settled, bottom = settle_part(edge_x, (x_left, x_right))
    out = micro_part(edge_x, settled, inflow(bottom), (inner,))
    return out.reshape(field.shape)


def solution(mesh):
    cells = P("gz", "gx", "gy")
    return jax.shard_map(
        shards,
        mesh=mesh,
        in_specs=(P(None, "gz", "gx", "gy"), cells, cells, cells, cells) + (P(),) * 6,
        out_specs=P(None, "gz", "gx", "gy"),
        check_vma=False,
    )
```

```python
import functools

import jax
import jax.numpy as jnp
from jax import lax
from jax.experimental import pallas as pl
from jax.experimental.pallas import tpu as pltpu
from jax.sharding import PartitionSpec as P

LANES = 128
SUB = 8
GROUP = 8


def roll_to(value, source, dest):
    shift = (dest - source) % LANES
    return value if shift == 0 else pltpu.roll(value, shift, 1)


def pack_x_kernel(nx, field_ref, right_ref, left_ref):
    rows = field_ref.shape[1]
    for b in range(field_ref.shape[0]):
        right_ref[b] = field_ref[b, pl.ds(nx - 1, rows // nx, stride=nx), :]
        left_ref[b] = field_ref[b, pl.ds(0, rows // nx, stride=nx), :]


def pack_y_kernel(nx, field_ref, cour_ref, right_ref, left_ref):
    _, rows, _ = field_ref.shape
    per_bin = rows // SUB
    blocks = rows // (SUB * nx)
    lane = lax.broadcasted_iota(jnp.int32, (SUB, LANES), 1)

    def one(load, offset, packed):
        for x in range(nx):
            for q in range(blocks):
                at = offset + x * blocks + q
                value = load(pl.ds(q * SUB * nx + x, SUB, stride=nx))
                hit = lane == at
                packed = (
                    jnp.where(hit, roll_to(value, LANES - 1, at), packed[0]),
                    jnp.where(hit, roll_to(value, 0, at), packed[1]),
                )
        return packed

    zero = jnp.zeros((SUB, LANES), jnp.float32)
    step = pl.program_id(0)
    final = pl.num_programs(0) - 1

    @pl.when(step < final)
    def _():
        packed = (zero, zero)
        for k in range(GROUP):
            packed = one(lambda r: field_ref[k, r, :], k * per_bin, packed)
        right_ref[0] = packed[0]
        left_ref[0] = packed[1]

    @pl.when(step == final)
    def _():
        right_ref[0] = one(lambda r: cour_ref[r, :], 0, (zero, zero))[0]


def advect_settle_kernel(nx, xs, halos, *refs):
    if halos:
        scal, field, cx, cy, yl, yr, table, cl, xl, xr, out, bottom = refs
    else:
        scal, field, cx, cy, yl, yr, table, out, bottom = refs
        cl = xl = xr = None
    bins, rows, _ = field.shape
    blocks = rows // (SUB * nx)
    per_bin = nx * blocks
    lane = lax.broadcasted_iota(jnp.int32, (SUB, LANES), 1)
    first, last = lane == 0, lane == LANES - 1
    for xi, x in enumerate(xs):
        for q in reversed(range(blocks)):
            span = lambda xx: pl.ds(q * SUB * nx + xx, SUB, stride=nx)
            spot = x * blocks + q
            zrows = pl.ds(q * SUB, SUB)
            c_here = cx[span(x), :]
            c_left = cx[span(x - 1), :] if x > 0 else cl[zrows, :]
            y_here = cy[span(x), :]
            y_left = jnp.where(
                first, roll_to(yl[bins // GROUP], spot, 0), pltpu.roll(y_here, 1, 1)
            )
            stay = (
                1.0
                - jnp.maximum(c_here, 0.0)
                + jnp.minimum(c_left, 0.0)
                - jnp.maximum(y_here, 0.0)
                + jnp.minimum(y_left, 0.0)
            )
            from_right = -jnp.minimum(c_here, 0.0)
            from_left = jnp.maximum(c_left, 0.0)
            from_up = -jnp.minimum(y_here, 0.0)
            from_down = jnp.maximum(y_left, 0.0)

            def group(g, _):
                down_pack = yl[g]
                up_pack = yr[g]
                moved, falls = [], []
                for k in range(GROUP):
                    b = g * GROUP + k
                    here = field[b, span(x), :]
                    left = field[b, span(x - 1), :] if x > 0 else xl[b, zrows, :]
                    right = field[b, span(x + 1), :] if x < nx - 1 else xr[b, zrows, :]
                    at = k * per_bin + spot
                    down = jnp.where(first, roll_to(down_pack, at, 0), pltpu.roll(here, 1, 1))
                    up = jnp.where(
                        last, roll_to(up_pack, at, LANES - 1), pltpu.roll(here, LANES - 1, 1)
                    )
                    moved.append(
                        stay * here
                        + from_right * right
                        + from_left * left
                        + from_up * up
                        + from_down * down
                    )
                for k in range(GROUP):
                    b = g * GROUP + k
                    fall = moved[k] * scal[b]
                    fall = fall + table[b, 0] * pltpu.roll(fall, SUB - 1, 0)
                    fall = fall + table[b, 1] * pltpu.roll(fall, SUB - 2, 0)
                    fall = fall + table[b, 2] * pltpu.roll(fall, SUB - 4, 0)
                    if q < blocks - 1:
                        above = out[b, xi * blocks + q + 1, pl.ds(0, 1), :]
                        fall = fall + table[b, 3] * above
                    falls.append(fall)
                for k in range(GROUP):
                    b = g * GROUP + k
                    out[b, xi * blocks + q] = falls[k]
                    if q == 0:
                        bottom[xi, pl.ds(b, 1), :] = falls[k][0:1, :]
                return 0

            lax.fori_loop(0, bins // GROUP, group, 0)


def micro_kernel(nx, xs, slots, merge, *refs):
    if merge:
        scal, index, settled, carry, table, sat_ref, mask_ref, inner, out, grown, change = refs
    else:
        scal, index, settled, carry, table, sat_ref, mask_ref, out, grown, change = refs
    bins = settled.shape[0]
    drops = grown.shape[0]
    aero = bins - drops
    cells = grown.shape[1]
    blocks = cells // len(xs)
    at_growth = bins + blocks * bins
    at_threshold = at_growth + drops
    at_rate = at_threshold + aero

    def spans(v):
        x, q = xs[v // blocks], v % blocks
        return pl.ds(q * SUB * nx + x, SUB, stride=nx)

    sat = [sat_ref[spans(v), :] for v in range(cells)]

    def full(b):
        values = []
        decay = table[b, 3]
        for v in range(cells):
            xi, q = v // blocks, v % blocks
            values.append(
                settled[b, v]
                + (decay * scal[bins + q * bins + b]) * carry[xi, pl.ds(b, 1), :]
            )
        return values

    def put(b, v, value):
        if merge:
            out[b, spans(v), :] = value
        else:
            out[b, v] = value

    zero = jnp.zeros((SUB, LANES), jnp.float32)

    def activate(j, gained):
        mass = full(drops + j)
        fresh = []
        for v in range(cells):
            active = jnp.maximum(sat[v] - scal[at_threshold + j], 0.0) * mass[v]
            put(drops + j, v, mass[v] - active)
            fresh.append(gained[v] + active)
        return tuple(fresh)

    gained = lax.fori_loop(0, aero, activate, (zero,) * cells)

    def condense(b, state):
        current, below = state
        after = full(b + 1)
        flux = []
        for v in range(cells):
            face = scal[at_growth + b] * sat[v]
            flux.append(jnp.maximum(face, 0.0) * current[v] + jnp.minimum(face, 0.0) * after[v])
            grown[b, v] = current[v] + below[v] - flux[v]
            change[b, v] = zero
        return tuple(after), tuple(flux)

    current, below = lax.fori_loop(
        0, drops - 1, condense, (tuple(full(0)), (zero,) * cells)
    )
    for v in range(cells):
        grown[drops - 1, v] = current[v] + below[v]
        change[drops - 1, v] = zero
        grown[0, v] = grown[0, v] + gained[v]

    def collide(i, _):
        mine = grown[i]
        loss = jnp.zeros_like(mine)
        for m in range(slots):
            pair = i * slots + m
            rate = (mine * scal[at_rate + pair]) * grown[index[pair]]
            loss = loss + rate
            goal = index[drops * slots + pair]
            change[goal] = change[goal] + rate
        change[i] = change[i] - loss
        return 0

    lax.fori_loop(0, drops, collide, 0)

    mask = [mask_ref[spans(v), :].astype(jnp.float32) for v in range(cells)]

    def finish(b, _):
        for v in range(cells):
            put(b, v, grown[b, v] + mask[v] * change[b, v])
        return 0

    lax.fori_loop(0, drops, finish, 0)

    if merge:
        others = [x for x in range(nx) if x not in xs]

        def fill(b, _):
            for xi, x in enumerate(others):
                for q in range(blocks):
                    out[b, pl.ds(q * SUB * nx + x, SUB, stride=nx), :] = inner[b, xi * blocks + q]
            return 0

        lax.fori_loop(0, bins, fill, 0)


VMEM = pl.BlockSpec(memory_space=pltpu.VMEM)
SMEM = pl.BlockSpec(memory_space=pltpu.SMEM)
PARAMS = pltpu.CompilerParams(vmem_limit_bytes=48 * 1024 * 1024)


def cost(flops, bytes_accessed):
    return pl.CostEstimate(flops=flops, bytes_accessed=bytes_accessed, transcendentals=0)


def shift_up(value, axis):
    count = lax.axis_size(axis)
    return lax.ppermute(value, axis, [(i, (i + 1) % count) for i in range(count)])


def shift_down(value, axis):
    count = lax.axis_size(axis)
    return lax.ppermute(value, axis, [((i + 1) % count, i) for i in range(count)])


def shards(
    field,
    courant_x,
    courant_y,
    supersat,
    cloud_mask,
    fall_speed,
    growth,
    activation_threshold,
    kernel_rate,
    partner,
    target,
):
    bins, depth, nx, ny = field.shape
    drops, slots = partner.shape
    f32 = jnp.float32
    blocks = depth // SUB
    flat = field.reshape(bins, depth * nx, ny)
    cx, cy, sat, mask = (
        a.reshape(depth * nx, ny) for a in (courant_x, courant_y, supersat, cloud_mask)
    )

    groups = bins // GROUP
    face = jax.ShapeDtypeStruct((bins, depth, ny), f32)
    to_right, to_left = pl.pallas_call(
        functools.partial(pack_x_kernel, nx),
        grid=(groups,),
        out_shape=(face, face),
        in_specs=[pl.BlockSpec((GROUP, depth * nx, ny), lambda g: (g, 0, 0))],
        out_specs=(pl.BlockSpec((GROUP, depth, ny), lambda g: (g, 0, 0)),) * 2,
        compiler_params=PARAMS,
        cost_estimate=cost(1 << 20, 6 << 20),
        name="pack_x",
    )(flat)
    x_left = shift_up(to_right, "gx")
    x_right = shift_down(to_left, "gx")
    cx_left = shift_up(courant_x[:, nx - 1, :], "gx")
    flat_y, _, _ = lax.optimization_barrier((flat, to_right, to_left))

    y_to_right, y_to_left = pl.pallas_call(
        functools.partial(pack_y_kernel, nx),
        grid=(groups + 1,),
        out_shape=(
            jax.ShapeDtypeStruct((groups + 1, SUB, LANES), f32),
            jax.ShapeDtypeStruct((groups, SUB, LANES), f32),
        ),
        in_specs=[
            pl.BlockSpec((GROUP, depth * nx, ny), lambda g: (jnp.minimum(g, groups - 1), 0, 0)),
            pl.BlockSpec((depth * nx, ny), lambda g: (0, 0)),
        ],
        out_specs=(
            pl.BlockSpec((1, SUB, LANES), lambda g: (g, 0, 0)),
            pl.BlockSpec((1, SUB, LANES), lambda g: (jnp.minimum(g, groups - 1), 0, 0)),
        ),
        compiler_params=PARAMS,
        cost_estimate=cost(1 << 22, 1 << 22),
        name="pack_y",
    )(flat_y, cy)
    y_left = shift_up(y_to_right, "gy")
    y_right = shift_down(y_to_left, "gy")

    ratio = fall_speed / (1.0 + fall_speed)
    log_ratio = jnp.log(ratio)
    sub = jnp.arange(SUB, dtype=f32)
    power = jnp.stack([jnp.full((SUB,), 1.0, f32), jnp.full((SUB,), 2.0, f32), jnp.full((SUB,), 4.0, f32), SUB - sub])
    keep = jnp.stack([sub < SUB - 1, sub < SUB - 2, sub < SUB - 4, sub < SUB])
    table = jnp.where(keep, jnp.exp(log_ratio[:, None, None] * power), 0.0)
    table = jnp.broadcast_to(table[..., None], (bins, 4, SUB, LANES))
    step = jnp.exp(log_ratio[None, :] * (SUB * jnp.arange(blocks - 1, -1, -1, dtype=f32))[:, None])
    scal = jnp.concatenate(
        [
            1.0 / (1.0 + fall_speed),
            step.reshape(-1),
            growth,
            jnp.zeros((1,), f32),
            activation_threshold,
            kernel_rate.reshape(-1),
        ]
    )
    index = jnp.concatenate([partner.reshape(-1), target.reshape(-1)])

    inner_x = tuple(range(1, nx - 1))
    edge_x = (0, nx - 1)

    def settle_part(xs, halos):
        cells = len(xs) * blocks
        args = [scal, flat, cx, cy, y_left, y_right, table] + list(halos)
        return pl.pallas_call(
            functools.partial(advect_settle_kernel, nx, xs, bool(halos)),
            out_shape=(
                jax.ShapeDtypeStruct((bins, cells, SUB, LANES), f32),
                jax.ShapeDtypeStruct((len(xs), bins, LANES), f32),
            ),
            in_specs=[SMEM] + [VMEM] * (len(args) - 1),
            out_specs=(VMEM, VMEM),
            compiler_params=PARAMS,
            cost_estimate=cost(1 << 24, 8 << 20),
            name="settle_edge" if halos else "settle_inner",
        )(*args)

    count = lax.axis_size("gz")
    whole = jnp.exp(log_ratio * depth)[None, :, None]

    def inflow(bottom):
        carry = jnp.zeros_like(bottom)
        for hop in range(count - 1):
            sent = bottom if hop == 0 else bottom + whole * carry
            carry = lax.ppermute(sent, "gz", [(i + 1, i) for i in range(count - 1)])
        return carry

    def micro_part(xs, settled, carry, inner):
        cells = len(xs) * blocks
        args = [scal, index, settled, carry, table, sat, mask] + list(inner)
        if inner:
            out = jax.ShapeDtypeStruct((bins, depth * nx, ny), f32)
        else:
            out = jax.ShapeDtypeStruct((bins, cells, SUB, LANES), f32)
        return pl.pallas_call(
            functools.partial(micro_kernel, nx, xs, slots, bool(inner)),
            out_shape=out,
            in_specs=[SMEM, SMEM] + [VMEM] * (len(args) - 2),
            out_specs=VMEM,
            scratch_shapes=[
                pltpu.VMEM((drops, cells, SUB, LANES), f32),
                pltpu.VMEM((drops, cells, SUB, LANES), f32),
            ],
            compiler_params=PARAMS,
            cost_estimate=cost(1 << 24, 8 << 20),
            name="micro_edge" if inner else "micro_inner",
        )(*args)

    settled, bottom = settle_part(inner_x, ())
    inner = micro_part(inner_x, settled, inflow(bottom), ())
    x_left, x_right, inner = lax.optimization_barrier((x_left, x_right, inner))
    settled, bottom = settle_part(edge_x, (cx_left, x_left, x_right))
    out = micro_part(edge_x, settled, inflow(bottom), (inner,))
    return out.reshape(field.shape)


def solution(mesh):
    cells = P("gz", "gx", "gy")
    return jax.shard_map(
        shards,
        mesh=mesh,
        in_specs=(P(None, "gz", "gx", "gy"), cells, cells, cells, cells) + (P(),) * 6,
        out_specs=P(None, "gz", "gx", "gy"),
        check_vma=False,
    )
```

```python
import functools

import jax
import jax.numpy as jnp
from jax import lax
from jax.experimental import pallas as pl
from jax.experimental.pallas import tpu as pltpu
from jax.sharding import PartitionSpec as P

LANES = 128
SUB = 8
GROUP = 8


def roll_to(value, source, dest):
    shift = (dest - source) % LANES
    return value if shift == 0 else pltpu.roll(value, shift, 1)


def pack_y_kernel(nx, field_ref, cour_ref, right_ref, left_ref):
    _, rows, _ = field_ref.shape
    per_bin = rows // SUB
    blocks = rows // (SUB * nx)
    lane = lax.broadcasted_iota(jnp.int32, (SUB, LANES), 1)

    def one(load, offset, packed):
        for x in range(nx):
            for q in range(blocks):
                at = offset + x * blocks + q
                value = load(pl.ds(q * SUB * nx + x, SUB, stride=nx))
                hit = lane == at
                packed = (
                    jnp.where(hit, roll_to(value, LANES - 1, at), packed[0]),
                    jnp.where(hit, roll_to(value, 0, at), packed[1]),
                )
        return packed

    zero = jnp.zeros((SUB, LANES), jnp.float32)
    step = pl.program_id(0)
    final = pl.num_programs(0) - 1

    @pl.when(step < final)
    def _():
        packed = (zero, zero)
        for k in range(GROUP):
            packed = one(lambda r: field_ref[k, r, :], k * per_bin, packed)
        right_ref[0] = packed[0]
        left_ref[0] = packed[1]

    @pl.when(step == final)
    def _():
        right_ref[0] = one(lambda r: cour_ref[r, :], 0, (zero, zero))[0]


def scan_levels(value, table, b):
    value = value + table[b, 0] * pltpu.roll(value, SUB - 1, 0)
    value = value + table[b, 1] * pltpu.roll(value, SUB - 2, 0)
    return value + table[b, 2] * pltpu.roll(value, SUB - 4, 0)


def settle_kernel(nx, sets, *refs):
    scal, field, cx, cy, yl, yr, table = refs[:7]
    outs = refs[7:]
    bins, rows, _ = field.shape
    blocks = rows // (SUB * nx)
    per_bin = nx * blocks
    lane = lax.broadcasted_iota(jnp.int32, (SUB, LANES), 1)
    first, last = lane == 0, lane == LANES - 1
    places = [
        (x, xi, outs[2 * n], outs[2 * n + 1]) for n, xs in enumerate(sets) for xi, x in enumerate(xs)
    ]
    for x, xi, out, bottom in places:
        for q in reversed(range(blocks)):
            span = lambda xx: pl.ds(q * SUB * nx + xx, SUB, stride=nx)
            spot = x * blocks + q
            c_here = cx[span(x), :]
            y_here = cy[span(x), :]
            y_left = jnp.where(
                first, roll_to(yl[bins // GROUP], spot, 0), pltpu.roll(y_here, 1, 1)
            )
            stay = (
                1.0
                - jnp.maximum(c_here, 0.0)
                - jnp.maximum(y_here, 0.0)
                + jnp.minimum(y_left, 0.0)
            )
            if x > 0:
                c_left = cx[span(x - 1), :]
                stay = stay + jnp.minimum(c_left, 0.0)
                from_left = jnp.maximum(c_left, 0.0)
            from_right = -jnp.minimum(c_here, 0.0)
            from_up = -jnp.minimum(y_here, 0.0)
            from_down = jnp.maximum(y_left, 0.0)

            def group(g, _):
                down_pack = yl[g]
                up_pack = yr[g]
                falls = []
                for k in range(GROUP):
                    b = g * GROUP + k
                    here = field[b, span(x), :]
                    at = k * per_bin + spot
                    down = jnp.where(first, roll_to(down_pack, at, 0), pltpu.roll(here, 1, 1))
                    up = jnp.where(
                        last, roll_to(up_pack, at, LANES - 1), pltpu.roll(here, LANES - 1, 1)
                    )
                    moved = stay * here + from_up * up + from_down * down
                    if x > 0:
                        moved = moved + from_left * field[b, span(x - 1), :]
                    if x < nx - 1:
                        moved = moved + from_right * field[b, span(x + 1), :]
                    fall = scan_levels(moved * scal[b], table, b)
                    if q < blocks - 1:
                        fall = fall + table[b, 3] * out[b, xi * blocks + q + 1, pl.ds(0, 1), :]
                    falls.append(fall)
                for k in range(GROUP):
                    b = g * GROUP + k
                    out[b, xi * blocks + q] = falls[k]
                    if q == 0:
                        bottom[xi, pl.ds(b, 1), :] = falls[k][0:1, :]
                return 0

            lax.fori_loop(0, bins // GROUP, group, 0)


def edge_kernel(nx, *refs):
    scal, part, part_bottom, cx, table, cl, own, xl, xr, out, bottom = refs
    bins, cells = part.shape[:2]
    blocks = cells // 2
    leaves = [jnp.minimum(cl[pl.ds(q * SUB, SUB), :], 0.0) for q in range(blocks)]
    enters = [jnp.maximum(cl[pl.ds(q * SUB, SUB), :], 0.0) for q in range(blocks)]
    backs = [
        -jnp.minimum(cx[pl.ds(q * SUB * nx + nx - 1, SUB, stride=nx), :], 0.0)
        for q in range(blocks)
    ]

    def group(g, _):
        values, ends = [], []
        for k in range(4):
            b = g * 4 + k
            for xi in range(2):
                above = None
                for q in reversed(range(blocks)):
                    zrows = pl.ds(q * SUB, SUB)
                    if xi == 0:
                        flux = enters[q] * xl[b, zrows, :] + leaves[q] * own[b, zrows, :]
                    else:
                        flux = backs[q] * xr[b, zrows, :]
                    fall = scan_levels(flux * scal[b], table, b)
                    if above is not None:
                        fall = fall + table[b, 3] * above
                    above = fall[0:1, :]
                    values.append((b, xi * blocks + q, fall + part[b, xi * blocks + q]))
                ends.append((xi, b, above + part_bottom[xi, pl.ds(b, 1), :]))
        for b, v, value in values:
            out[b, v] = value
        for xi, b, value in ends:
            bottom[xi, pl.ds(b, 1), :] = value
        return 0

    lax.fori_loop(0, bins // 4, group, 0)


def micro_kernel(nx, xs, slots, merge, *refs):
    if merge:
        scal, index, settled, carry, table, sat_ref, mask_ref, inner, out, grown, change = refs
    else:
        scal, index, settled, carry, table, sat_ref, mask_ref, out, grown, change = refs
    bins = settled.shape[0]
    drops = grown.shape[0]
    aero = bins - drops
    cells = grown.shape[1]
    blocks = cells // len(xs)
    at_growth = bins + blocks * bins
    at_threshold = at_growth + drops
    at_rate = at_threshold + aero

    def spans(v):
        x, q = xs[v // blocks], v % blocks
        return pl.ds(q * SUB * nx + x, SUB, stride=nx)

    sat = [sat_ref[spans(v), :] for v in range(cells)]

    def full(b):
        values = []
        decay = table[b, 3]
        for v in range(cells):
            xi, q = v // blocks, v % blocks
            values.append(
                settled[b, v]
                + (decay * scal[bins + q * bins + b]) * carry[xi, pl.ds(b, 1), :]
            )
        return values

    def put(b, v, value):
        if merge:
            out[b, spans(v), :] = value
        else:
            out[b, v] = value

    zero = jnp.zeros((SUB, LANES), jnp.float32)

    def activate(j, gained):
        mass = full(drops + j)
        fresh = []
        for v in range(cells):
            active = jnp.maximum(sat[v] - scal[at_threshold + j], 0.0) * mass[v]
            put(drops + j, v, mass[v] - active)
            fresh.append(gained[v] + active)
        return tuple(fresh)

    gained = lax.fori_loop(0, aero, activate, (zero,) * cells)

    def condense(b, state):
        current, below = state
        after = full(b + 1)
        flux = []
        for v in range(cells):
            face = scal[at_growth + b] * sat[v]
            flux.append(jnp.maximum(face, 0.0) * current[v] + jnp.minimum(face, 0.0) * after[v])
            grown[b, v] = current[v] + below[v] - flux[v]
            change[b, v] = zero
        return tuple(after), tuple(flux)

    current, below = lax.fori_loop(
        0, drops - 1, condense, (tuple(full(0)), (zero,) * cells)
    )
    for v in range(cells):
        grown[drops - 1, v] = current[v] + below[v]
        change[drops - 1, v] = zero
        grown[0, v] = grown[0, v] + gained[v]

    def collide(i, _):
        mine = grown[i]
        loss = jnp.zeros_like(mine)
        for m in range(slots):
            pair = i * slots + m
            rate = (mine * scal[at_rate + pair]) * grown[index[pair]]
            loss = loss + rate
            goal = index[drops * slots + pair]
            change[goal] = change[goal] + rate
        change[i] = change[i] - loss
        return 0

    lax.fori_loop(0, drops, collide, 0)

    mask = [mask_ref[spans(v), :].astype(jnp.float32) for v in range(cells)]

    def finish(b, _):
        for v in range(cells):
            put(b, v, grown[b, v] + mask[v] * change[b, v])
        return 0

    lax.fori_loop(0, drops, finish, 0)

    if merge:
        others = [x for x in range(nx) if x not in xs]

        def fill(b, _):
            for xi, x in enumerate(others):
                for q in range(blocks):
                    out[b, pl.ds(q * SUB * nx + x, SUB, stride=nx), :] = inner[b, xi * blocks + q]
            return 0

        lax.fori_loop(0, bins, fill, 0)


VMEM = pl.BlockSpec(memory_space=pltpu.VMEM)
SMEM = pl.BlockSpec(memory_space=pltpu.SMEM)
PARAMS = pltpu.CompilerParams(vmem_limit_bytes=48 * 1024 * 1024)


def cost(flops, bytes_accessed):
    return pl.CostEstimate(flops=flops, bytes_accessed=bytes_accessed, transcendentals=0)


def shift_up(value, axis):
    count = lax.axis_size(axis)
    return lax.ppermute(value, axis, [(i, (i + 1) % count) for i in range(count)])


def shift_down(value, axis):
    count = lax.axis_size(axis)
    return lax.ppermute(value, axis, [((i + 1) % count, i) for i in range(count)])


def shards(
    field,
    courant_x,
    courant_y,
    supersat,
    cloud_mask,
    fall_speed,
    growth,
    activation_threshold,
    kernel_rate,
    partner,
    target,
):
    bins, depth, nx, ny = field.shape
    drops, slots = partner.shape
    f32 = jnp.float32
    blocks = depth // SUB
    flat = field.reshape(bins, depth * nx, ny)
    cx, cy, sat, mask = (
        a.reshape(depth * nx, ny) for a in (courant_x, courant_y, supersat, cloud_mask)
    )

    groups = bins // GROUP
    to_right, to_left = field[:, :, nx - 1, :], field[:, :, 0, :]
    x_left = shift_up(to_right, "gx")
    x_right = shift_down(to_left, "gx")
    flat_y, cx_last, to_right, to_left = lax.optimization_barrier((flat, courant_x, to_right, to_left))
    cx_left = shift_up(cx_last[:, nx - 1, :], "gx")

    y_to_right, y_to_left = pl.pallas_call(
        functools.partial(pack_y_kernel, nx),
        grid=(groups + 1,),
        out_shape=(
            jax.ShapeDtypeStruct((groups + 1, SUB, LANES), f32),
            jax.ShapeDtypeStruct((groups, SUB, LANES), f32),
        ),
        in_specs=[
            pl.BlockSpec((GROUP, depth * nx, ny), lambda g: (jnp.minimum(g, groups - 1), 0, 0)),
            pl.BlockSpec((depth * nx, ny), lambda g: (0, 0)),
        ],
        out_specs=(
            pl.BlockSpec((1, SUB, LANES), lambda g: (g, 0, 0)),
            pl.BlockSpec((1, SUB, LANES), lambda g: (jnp.minimum(g, groups - 1), 0, 0)),
        ),
        compiler_params=PARAMS,
        cost_estimate=cost(1 << 22, 1 << 22),
        name="pack_y",
    )(flat_y, cy)
    y_left = shift_up(y_to_right, "gy")
    y_right = shift_down(y_to_left, "gy")

    ratio = fall_speed / (1.0 + fall_speed)
    log_ratio = jnp.log(ratio)
    sub = jnp.arange(SUB, dtype=f32)
    power = jnp.stack([jnp.full((SUB,), 1.0, f32), jnp.full((SUB,), 2.0, f32), jnp.full((SUB,), 4.0, f32), SUB - sub])
    keep = jnp.stack([sub < SUB - 1, sub < SUB - 2, sub < SUB - 4, sub < SUB])
    table = jnp.where(keep, jnp.exp(log_ratio[:, None, None] * power), 0.0)
    table = jnp.broadcast_to(table[..., None], (bins, 4, SUB, LANES))
    step = jnp.exp(log_ratio[None, :] * (SUB * jnp.arange(blocks - 1, -1, -1, dtype=f32))[:, None])
    scal = jnp.concatenate(
        [
            1.0 / (1.0 + fall_speed),
            step.reshape(-1),
            growth,
            jnp.zeros((1,), f32),
            activation_threshold,
            kernel_rate.reshape(-1),
        ]
    )
    index = jnp.concatenate([partner.reshape(-1), target.reshape(-1)])

    inner_x = tuple(range(1, nx - 1))
    edge_x = (0, nx - 1)

    def settle_shapes(xs):
        return (
            jax.ShapeDtypeStruct((bins, len(xs) * blocks, SUB, LANES), f32),
            jax.ShapeDtypeStruct((len(xs), bins, LANES), f32),
        )

    count = lax.axis_size("gz")
    whole = jnp.exp(log_ratio * depth)[None, :, None]

    def inflow(bottom):
        carry = jnp.zeros_like(bottom)
        for hop in range(count - 1):
            sent = bottom if hop == 0 else bottom + whole * carry
            carry = lax.ppermute(sent, "gz", [(i + 1, i) for i in range(count - 1)])
        return carry

    def micro_part(xs, settled, carry, inner):
        cells = len(xs) * blocks
        args = [scal, index, settled, carry, table, sat, mask] + list(inner)
        if inner:
            out = jax.ShapeDtypeStruct((bins, depth * nx, ny), f32)
        else:
            out = jax.ShapeDtypeStruct((bins, cells, SUB, LANES), f32)
        return pl.pallas_call(
            functools.partial(micro_kernel, nx, xs, slots, bool(inner)),
            out_shape=out,
            in_specs=[SMEM, SMEM] + [VMEM] * (len(args) - 2),
            out_specs=VMEM,
            scratch_shapes=[
                pltpu.VMEM((drops, cells, SUB, LANES), f32),
                pltpu.VMEM((drops, cells, SUB, LANES), f32),
            ],
            compiler_params=PARAMS,
            cost_estimate=cost(1 << 24, 8 << 20),
            name="micro_edge" if inner else "micro_inner",
        )(*args)

    settled, bottom, part, part_bottom = pl.pallas_call(
        functools.partial(settle_kernel, nx, (inner_x, edge_x)),
        out_shape=settle_shapes(inner_x) + settle_shapes(edge_x),
        in_specs=[SMEM] + [VMEM] * 6,
        out_specs=(VMEM,) * 4,
        compiler_params=PARAMS,
        cost_estimate=cost(1 << 24, 16 << 20),
        name="settle_all",
    )(scal, flat_y, cx, cy, y_left, y_right, table)
    inner_carry = inflow(bottom)
    edge_settled, edge_bottom = pl.pallas_call(
        functools.partial(edge_kernel, nx),
        out_shape=settle_shapes(edge_x),
        in_specs=[SMEM] + [VMEM] * 8,
        out_specs=(VMEM,) * 2,
        compiler_params=PARAMS,
        cost_estimate=cost(1 << 23, 8 << 20),
        name="settle_edge",
    )(scal, part, part_bottom, cx, table, cx_left, to_left, x_left, x_right)
    settled, edge_bottom = lax.optimization_barrier((settled, edge_bottom))
    edge_carry = inflow(edge_bottom)
    inner = micro_part(inner_x, settled, inner_carry, ())
    out = micro_part(edge_x, edge_settled, edge_carry, (inner,))
    return out.reshape(field.shape)


def solution(mesh):
    cells = P("gz", "gx", "gy")
    return jax.shard_map(
        shards,
        mesh=mesh,
        in_specs=(P(None, "gz", "gx", "gy"), cells, cells, cells, cells) + (P(),) * 6,
        out_specs=P(None, "gz", "gx", "gy"),
        check_vma=False,
    )
```

```python
import functools

import jax
import jax.numpy as jnp
from jax import lax
from jax.experimental import pallas as pl
from jax.experimental.pallas import tpu as pltpu
from jax.sharding import PartitionSpec as P

LANES = 128
SUB = 8
GROUP = 8


def roll_to(value, source, dest):
    shift = (dest - source) % LANES
    return value if shift == 0 else pltpu.roll(value, shift, 1)


def lane_of(at):
    return 2 * (at % (LANES // 2)) + at // (LANES // 2)


def pack_y_kernel(nx, field_ref, cour_ref, right_ref, left_ref):
    bins, rows, _ = field_ref.shape
    per_bin = rows // SUB
    blocks = rows // (SUB * nx)
    lane = lax.broadcasted_iota(jnp.int32, (SUB, LANES), 1)

    def one(load, offset, packed):
        for x in range(nx):
            for q in range(blocks):
                at = lane_of(offset + x * blocks + q)
                under = (at - 1) % LANES
                value = load(pl.ds(q * SUB * nx + x, SUB, stride=nx))
                packed = (
                    jnp.where(lane == at, roll_to(value, LANES - 1, at), packed[0]),
                    jnp.where(lane == under, roll_to(value, 0, under), packed[1]),
                )
        return packed

    zero = jnp.zeros((SUB, LANES), jnp.float32)

    def group(g, _):
        packed = (zero, zero)
        for k in range(GROUP):
            packed = one(lambda r: field_ref[g * GROUP + k, r, :], k * per_bin, packed)
        right_ref[g] = packed[0]
        left_ref[g] = packed[1]
        return 0

    lax.fori_loop(0, bins // GROUP, group, 0)
    right_ref[bins // GROUP] = one(lambda r: cour_ref[r, :], 0, (zero, zero))[0]


def scan_levels(value, table, b):
    value = value + table[b, 0] * pltpu.roll(value, SUB - 1, 0)
    value = value + table[b, 1] * pltpu.roll(value, SUB - 2, 0)
    return value + table[b, 2] * pltpu.roll(value, SUB - 4, 0)


def settle_kernel(nx, sets, *refs):
    scal, field, cx, cy, yl, yr, table = refs[:7]
    outs = refs[7:]
    bins, rows, _ = field.shape
    blocks = rows // (SUB * nx)
    per_bin = nx * blocks
    lane = lax.broadcasted_iota(jnp.int32, (SUB, LANES), 1)
    first, last = lane == 0, lane == LANES - 1
    even = lane % 2 == 0
    place = {x: (n, xi) for n, xs in enumerate(sets) for xi, x in enumerate(xs)}
    half = GROUP // 2
    for q in reversed(range(blocks)):
        spans = [pl.ds(q * SUB * nx + x, SUB, stride=nx) for x in range(nx)]
        c_all = [cx[spans[x], :] for x in range(nx)]
        stay, from_up, from_down = [], [], []
        for x in range(nx):
            y_here = cy[spans[x], :]
            edge = roll_to(yl[bins // GROUP], lane_of(x * blocks + q), 0)
            y_left = jnp.where(first, edge, pltpu.roll(y_here, 1, 1))
            kept = (
                1.0
                - jnp.maximum(c_all[x], 0.0)
                - jnp.maximum(y_here, 0.0)
                + jnp.minimum(y_left, 0.0)
            )
            if x > 0:
                kept = kept + jnp.minimum(c_all[x - 1], 0.0)
            stay.append(kept)
            from_up.append(-jnp.minimum(y_here, 0.0))
            from_down.append(jnp.maximum(y_left, 0.0))
        enters = [jnp.maximum(c, 0.0) for c in c_all]
        backs = [-jnp.minimum(c, 0.0) for c in c_all]

        def group(g, _):
            packs = (jnp.where(even, yl[g], yr[g]), jnp.where(even, yr[g], yl[g]))
            for part in range(2):
                falls = []
                for k in range(part * half, (part + 1) * half):
                    b = g * GROUP + k
                    row = [field[b, spans[x], :] for x in range(nx)]
                    for x in range(nx):
                        n, xi = place[x]
                        at = k * per_bin + x * blocks + q
                        halo = roll_to(packs[at // (LANES // 2)], lane_of(at), 0)
                        down = jnp.where(first, halo, pltpu.roll(row[x], 1, 1))
                        up = jnp.where(last, halo, pltpu.roll(row[x], LANES - 1, 1))
                        moved = stay[x] * row[x] + from_up[x] * up + from_down[x] * down
                        if x > 0:
                            moved = moved + enters[x - 1] * row[x - 1]
                        if x < nx - 1:
                            moved = moved + backs[x] * row[x + 1]
                        fall = scan_levels(moved * scal[b], table, b)
                        if q < blocks - 1:
                            above = outs[2 * n][b, xi * blocks + q + 1, pl.ds(0, 1), :]
                            fall = fall + table[b, 3] * above
                        falls.append((n, xi, b, fall))
                for n, xi, b, fall in falls:
                    outs[2 * n][b, xi * blocks + q] = fall
                    if q == 0:
                        outs[2 * n + 1][xi, pl.ds(b, 1), :] = fall[0:1, :]
            return 0

        lax.fori_loop(0, bins // GROUP, group, 0)


def edge_kernel(nx, *refs):
    scal, part, part_bottom, cx, table, cl, own, xl, xr, out, bottom = refs
    bins, cells = part.shape[:2]
    blocks = cells // 2
    leaves = [jnp.minimum(cl[pl.ds(q * SUB, SUB), :], 0.0) for q in range(blocks)]
    enters = [jnp.maximum(cl[pl.ds(q * SUB, SUB), :], 0.0) for q in range(blocks)]
    backs = [
        -jnp.minimum(cx[pl.ds(q * SUB * nx + nx - 1, SUB, stride=nx), :], 0.0)
        for q in range(blocks)
    ]

    def group(g, _):
        values, ends = [], []
        for k in range(4):
            b = g * 4 + k
            for xi in range(2):
                above = None
                for q in reversed(range(blocks)):
                    zrows = pl.ds(q * SUB, SUB)
                    if xi == 0:
                        flux = enters[q] * xl[b, zrows, :] + leaves[q] * own[b, zrows, :]
                    else:
                        flux = backs[q] * xr[b, zrows, :]
                    fall = scan_levels(flux * scal[b], table, b)
                    if above is not None:
                        fall = fall + table[b, 3] * above
                    above = fall[0:1, :]
                    values.append((b, xi * blocks + q, fall + part[b, xi * blocks + q]))
                ends.append((xi, b, above + part_bottom[xi, pl.ds(b, 1), :]))
        for b, v, value in values:
            out[b, v] = value
        for xi, b, value in ends:
            bottom[xi, pl.ds(b, 1), :] = value
        return 0

    lax.fori_loop(0, bins // 4, group, 0)


def micro_kernel(nx, xs, slots, merge, *refs):
    if merge:
        scal, index, settled, carry, table, sat_ref, mask_ref, inner, out, grown, change = refs
    else:
        scal, index, settled, carry, table, sat_ref, mask_ref, out, grown, change = refs
    bins = settled.shape[0]
    drops = grown.shape[0]
    aero = bins - drops
    cells = grown.shape[1]
    blocks = cells // len(xs)
    at_growth = bins + blocks * bins
    at_threshold = at_growth + drops
    at_rate = at_threshold + aero

    def spans(v):
        x, q = xs[v // blocks], v % blocks
        return pl.ds(q * SUB * nx + x, SUB, stride=nx)

    sat = [sat_ref[spans(v), :] for v in range(cells)]

    def full(b):
        values = []
        decay = table[b, 3]
        for v in range(cells):
            xi, q = v // blocks, v % blocks
            values.append(
                settled[b, v]
                + (decay * scal[bins + q * bins + b]) * carry[xi, pl.ds(b, 1), :]
            )
        return values

    def put(b, v, value):
        if merge:
            out[b, spans(v), :] = value
        else:
            out[b, v] = value

    zero = jnp.zeros((SUB, LANES), jnp.float32)

    def activate(j, gained):
        mass = full(drops + j)
        fresh = []
        for v in range(cells):
            active = jnp.maximum(sat[v] - scal[at_threshold + j], 0.0) * mass[v]
            put(drops + j, v, mass[v] - active)
            fresh.append(gained[v] + active)
        return tuple(fresh)

    gained = lax.fori_loop(0, aero, activate, (zero,) * cells)

    def condense(b, state):
        current, below = state
        after = full(b + 1)
        flux = []
        for v in range(cells):
            face = scal[at_growth + b] * sat[v]
            flux.append(jnp.maximum(face, 0.0) * current[v] + jnp.minimum(face, 0.0) * after[v])
            grown[b, v] = current[v] + below[v] - flux[v]
            change[b, v] = zero
        return tuple(after), tuple(flux)

    current, below = lax.fori_loop(
        0, drops - 1, condense, (tuple(full(0)), (zero,) * cells)
    )
    for v in range(cells):
        grown[drops - 1, v] = current[v] + below[v]
        change[drops - 1, v] = zero
        grown[0, v] = grown[0, v] + gained[v]

    def collide(i, _):
        mine = grown[i]
        loss = jnp.zeros_like(mine)
        for m in range(slots):
            pair = i * slots + m
            rate = (mine * scal[at_rate + pair]) * grown[index[pair]]
            loss = loss + rate
            goal = index[drops * slots + pair]
            change[goal] = change[goal] + rate
        change[i] = change[i] - loss
        return 0

    lax.fori_loop(0, drops, collide, 0)

    mask = [mask_ref[spans(v), :].astype(jnp.float32) for v in range(cells)]

    def finish(b, _):
        for v in range(cells):
            put(b, v, grown[b, v] + mask[v] * change[b, v])
        return 0

    lax.fori_loop(0, drops, finish, 0)

    if merge:
        others = [x for x in range(nx) if x not in xs]

        def fill(b, _):
            for xi, x in enumerate(others):
                for q in range(blocks):
                    out[b, pl.ds(q * SUB * nx + x, SUB, stride=nx), :] = inner[b, xi * blocks + q]
            return 0

        lax.fori_loop(0, bins, fill, 0)


VMEM = pl.BlockSpec(memory_space=pltpu.VMEM)
SMEM = pl.BlockSpec(memory_space=pltpu.SMEM)
PARAMS = pltpu.CompilerParams(vmem_limit_bytes=24 * 1024 * 1024)


def cost(flops, bytes_accessed):
    return pl.CostEstimate(flops=flops, bytes_accessed=bytes_accessed, transcendentals=0)


def shift_up(value, axis):
    count = lax.axis_size(axis)
    return lax.ppermute(value, axis, [(i, (i + 1) % count) for i in range(count)])


def shift_down(value, axis):
    count = lax.axis_size(axis)
    return lax.ppermute(value, axis, [((i + 1) % count, i) for i in range(count)])


def shards(
    field,
    courant_x,
    courant_y,
    supersat,
    cloud_mask,
    fall_speed,
    growth,
    activation_threshold,
    kernel_rate,
    partner,
    target,
):
    bins, depth, nx, ny = field.shape
    drops, slots = partner.shape
    f32 = jnp.float32
    blocks = depth // SUB
    flat = field.reshape(bins, depth * nx, ny)
    cx, cy, sat, mask = (
        a.reshape(depth * nx, ny) for a in (courant_x, courant_y, supersat, cloud_mask)
    )

    groups = bins // GROUP
    to_right, to_left = field[:, :, nx - 1, :], field[:, :, 0, :]
    x_left = shift_up(to_right, "gx")
    x_right = shift_down(to_left, "gx")
    cy, cx_last, to_right, to_left = lax.optimization_barrier((cy, courant_x, to_right, to_left))
    cx_left = shift_up(cx_last[:, nx - 1, :], "gx")

    y_to_right, y_to_left = pl.pallas_call(
        functools.partial(pack_y_kernel, nx),
        out_shape=(
            jax.ShapeDtypeStruct((groups + 1, SUB, LANES), f32),
            jax.ShapeDtypeStruct((groups, SUB, LANES), f32),
        ),
        in_specs=[VMEM, VMEM],
        out_specs=(VMEM, VMEM),
        compiler_params=PARAMS,
        cost_estimate=cost(1 << 22, 1 << 22),
        name="pack_y",
    )(flat, cy)
    y_left = shift_up(y_to_right, "gy")
    y_right = shift_down(y_to_left, "gy")

    ratio = fall_speed / (1.0 + fall_speed)
    log_ratio = jnp.log(ratio)
    sub = jnp.arange(SUB, dtype=f32)
    power = jnp.stack([jnp.full((SUB,), 1.0, f32), jnp.full((SUB,), 2.0, f32), jnp.full((SUB,), 4.0, f32), SUB - sub])
    keep = jnp.stack([sub < SUB - 1, sub < SUB - 2, sub < SUB - 4, sub < SUB])
    table = jnp.where(keep, jnp.exp(log_ratio[:, None, None] * power), 0.0)
    table = jnp.broadcast_to(table[..., None], (bins, 4, SUB, LANES))
    step = jnp.exp(log_ratio[None, :] * (SUB * jnp.arange(blocks - 1, -1, -1, dtype=f32))[:, None])
    scal = jnp.concatenate(
        [
            1.0 / (1.0 + fall_speed),
            step.reshape(-1),
            growth,
            jnp.zeros((1,), f32),
            activation_threshold,
            kernel_rate.reshape(-1),
        ]
    )
    index = jnp.concatenate([partner.reshape(-1), target.reshape(-1)])

    inner_x = tuple(range(1, nx - 1))
    edge_x = (0, nx - 1)

    def settle_shapes(xs):
        return (
            jax.ShapeDtypeStruct((bins, len(xs) * blocks, SUB, LANES), f32),
            jax.ShapeDtypeStruct((len(xs), bins, LANES), f32),
        )

    count = lax.axis_size("gz")
    whole = jnp.exp(log_ratio * depth)[None, :, None]

    def inflow(bottom):
        carry = jnp.zeros_like(bottom)
        for hop in range(count - 1):
            sent = bottom if hop == 0 else bottom + whole * carry
            carry = lax.ppermute(sent, "gz", [(i + 1, i) for i in range(count - 1)])
        return carry

    def micro_part(xs, settled, carry, inner):
        cells = len(xs) * blocks
        args = [scal, index, settled, carry, table, sat, mask] + list(inner)
        if inner:
            out = jax.ShapeDtypeStruct((bins, depth * nx, ny), f32)
        else:
            out = jax.ShapeDtypeStruct((bins, cells, SUB, LANES), f32)
        return pl.pallas_call(
            functools.partial(micro_kernel, nx, xs, slots, bool(inner)),
            out_shape=out,
            in_specs=[SMEM, SMEM] + [VMEM] * (len(args) - 2),
            out_specs=VMEM,
            scratch_shapes=[
                pltpu.VMEM((drops, cells, SUB, LANES), f32),
                pltpu.VMEM((drops, cells, SUB, LANES), f32),
            ],
            compiler_params=PARAMS,
            cost_estimate=cost(1 << 24, 8 << 20),
            name="micro_edge" if inner else "micro_inner",
        )(*args)

    settled, bottom, part, part_bottom = pl.pallas_call(
        functools.partial(settle_kernel, nx, (inner_x, edge_x)),
        out_shape=settle_shapes(inner_x) + settle_shapes(edge_x),
        in_specs=[SMEM] + [VMEM] * 6,
        out_specs=(VMEM,) * 4,
        compiler_params=PARAMS,
        cost_estimate=cost(1 << 24, 16 << 20),
        name="settle_all",
    )(scal, flat, cx, cy, y_left, y_right, table)
    inner_carry = inflow(bottom)
    edge_settled, edge_bottom = pl.pallas_call(
        functools.partial(edge_kernel, nx),
        out_shape=settle_shapes(edge_x),
        in_specs=[SMEM] + [VMEM] * 8,
        out_specs=(VMEM,) * 2,
        compiler_params=PARAMS,
        cost_estimate=cost(1 << 23, 8 << 20),
        name="settle_edge",
    )(scal, part, part_bottom, cx, table, cx_left, to_left, x_left, x_right)
    settled, edge_bottom = lax.optimization_barrier((settled, edge_bottom))
    edge_carry = inflow(edge_bottom)
    inner = micro_part(inner_x, settled, inner_carry, ())
    out = micro_part(edge_x, edge_settled, edge_carry, (inner,))
    return out.reshape(field.shape)


def solution(mesh):
    cells = P("gz", "gx", "gy")
    return jax.shard_map(
        shards,
        mesh=mesh,
        in_specs=(P(None, "gz", "gx", "gy"), cells, cells, cells, cells) + (P(),) * 6,
        out_specs=P(None, "gz", "gx", "gy"),
        check_vma=False,
    )
```

```python
import functools

import jax
import jax.numpy as jnp
from jax import lax
from jax.experimental import pallas as pl
from jax.experimental.pallas import tpu as pltpu
from jax.sharding import PartitionSpec as P

LANES = 128
SUB = 8
GROUP = 8


def roll_to(value, source, dest):
    shift = (dest - source) % LANES
    return value if shift == 0 else pltpu.roll(value, shift, 1)


def lane_of(at):
    return 2 * (at % (LANES // 2)) + at // (LANES // 2)


def pack_x_kernel(nx, field_ref, right_ref, left_ref):
    bins, rows, _ = field_ref.shape

    def group(g, _):
        for k in range(GROUP):
            b = g * GROUP + k
            for q in range(rows // (SUB * nx)):
                start = q * SUB * nx
                zrows = pl.ds(q * SUB, SUB)
                right_ref[b, zrows, :] = field_ref[b, pl.ds(start + nx - 1, SUB, stride=nx), :]
                left_ref[b, zrows, :] = field_ref[b, pl.ds(start, SUB, stride=nx), :]
        return 0

    lax.fori_loop(0, bins // GROUP, group, 0)


def pack_y_kernel(nx, field_ref, cour_ref, right_ref, left_ref):
    bins, rows, _ = field_ref.shape
    per_bin = rows // SUB
    blocks = rows // (SUB * nx)
    lane = lax.broadcasted_iota(jnp.int32, (SUB, LANES), 1)

    def one(load, offset, packed):
        for x in range(nx):
            for q in range(blocks):
                at = lane_of(offset + x * blocks + q)
                under = (at - 1) % LANES
                value = load(pl.ds(q * SUB * nx + x, SUB, stride=nx))
                packed = (
                    jnp.where(lane == at, roll_to(value, LANES - 1, at), packed[0]),
                    jnp.where(lane == under, roll_to(value, 0, under), packed[1]),
                )
        return packed

    zero = jnp.zeros((SUB, LANES), jnp.float32)

    def group(g, _):
        packed = (zero, zero)
        for k in range(GROUP):
            packed = one(lambda r: field_ref[g * GROUP + k, r, :], k * per_bin, packed)
        right_ref[g] = packed[0]
        left_ref[g] = packed[1]
        return 0

    lax.fori_loop(0, bins // GROUP, group, 0)
    right_ref[bins // GROUP] = one(lambda r: cour_ref[r, :], 0, (zero, zero))[0]


def scan_levels(value, table, b):
    value = value + table[b, 0] * pltpu.roll(value, SUB - 1, 0)
    value = value + table[b, 1] * pltpu.roll(value, SUB - 2, 0)
    return value + table[b, 2] * pltpu.roll(value, SUB - 4, 0)


def settle_kernel(nx, sets, *refs):
    scal, field, cx, cy, yl, yr, table = refs[:7]
    outs = refs[7:]
    bins, rows, _ = field.shape
    blocks = rows // (SUB * nx)
    per_bin = nx * blocks
    lane = lax.broadcasted_iota(jnp.int32, (SUB, LANES), 1)
    first, last = lane == 0, lane == LANES - 1
    even = lane % 2 == 0
    place = {x: (n, xi) for n, xs in enumerate(sets) for xi, x in enumerate(xs)}
    half = GROUP // 2
    for q in reversed(range(blocks)):
        spans = [pl.ds(q * SUB * nx + x, SUB, stride=nx) for x in range(nx)]
        c_all = [cx[spans[x], :] for x in range(nx)]
        stay, from_up, from_down = [], [], []
        for x in range(nx):
            y_here = cy[spans[x], :]
            edge = roll_to(yl[bins // GROUP], lane_of(x * blocks + q), 0)
            y_left = jnp.where(first, edge, pltpu.roll(y_here, 1, 1))
            kept = (
                1.0
                - jnp.maximum(c_all[x], 0.0)
                - jnp.maximum(y_here, 0.0)
                + jnp.minimum(y_left, 0.0)
            )
            if x > 0:
                kept = kept + jnp.minimum(c_all[x - 1], 0.0)
            stay.append(kept)
            from_up.append(-jnp.minimum(y_here, 0.0))
            from_down.append(jnp.maximum(y_left, 0.0))
        enters = [jnp.maximum(c, 0.0) for c in c_all]
        backs = [-jnp.minimum(c, 0.0) for c in c_all]

        def group(g, _):
            packs = (jnp.where(even, yl[g], yr[g]), jnp.where(even, yr[g], yl[g]))
            for part in range(2):
                falls = []
                for k in range(part * half, (part + 1) * half):
                    b = g * GROUP + k
                    row = [field[b, spans[x], :] for x in range(nx)]
                    for x in range(nx):
                        n, xi = place[x]
                        at = k * per_bin + x * blocks + q
                        halo = roll_to(packs[at // (LANES // 2)], lane_of(at), 0)
                        down = jnp.where(first, halo, pltpu.roll(row[x], 1, 1))
                        up = jnp.where(last, halo, pltpu.roll(row[x], LANES - 1, 1))
                        moved = stay[x] * row[x] + from_up[x] * up + from_down[x] * down
                        if x > 0:
                            moved = moved + enters[x - 1] * row[x - 1]
                        if x < nx - 1:
                            moved = moved + backs[x] * row[x + 1]
                        fall = scan_levels(moved * scal[b], table, b)
                        if q < blocks - 1:
                            above = outs[2 * n][b, xi * blocks + q + 1, pl.ds(0, 1), :]
                            fall = fall + table[b, 3] * above
                        falls.append((n, xi, b, fall))
                for n, xi, b, fall in falls:
                    outs[2 * n][b, xi * blocks + q] = fall
                    if q == 0:
                        outs[2 * n + 1][xi, pl.ds(b, 1), :] = fall[0:1, :]
            return 0

        lax.fori_loop(0, bins // GROUP, group, 0)


def edge_kernel(nx, *refs):
    scal, part, part_bottom, cx, table, cl, own, xl, xr, out, bottom = refs
    bins, cells = part.shape[:2]
    blocks = cells // 2
    leaves = [jnp.minimum(cl[pl.ds(q * SUB, SUB), :], 0.0) for q in range(blocks)]
    enters = [jnp.maximum(cl[pl.ds(q * SUB, SUB), :], 0.0) for q in range(blocks)]
    backs = [
        -jnp.minimum(cx[pl.ds(q * SUB * nx + nx - 1, SUB, stride=nx), :], 0.0)
        for q in range(blocks)
    ]

    def group(g, _):
        values, ends = [], []
        for k in range(4):
            b = g * 4 + k
            for xi in range(2):
                above = None
                for q in reversed(range(blocks)):
                    zrows = pl.ds(q * SUB, SUB)
                    if xi == 0:
                        flux = enters[q] * xl[b, zrows, :] + leaves[q] * own[b, zrows, :]
                    else:
                        flux = backs[q] * xr[b, zrows, :]
                    fall = scan_levels(flux * scal[b], table, b)
                    if above is not None:
                        fall = fall + table[b, 3] * above
                    above = fall[0:1, :]
                    values.append((b, xi * blocks + q, fall + part[b, xi * blocks + q]))
                ends.append((xi, b, above + part_bottom[xi, pl.ds(b, 1), :]))
        for b, v, value in values:
            out[b, v] = value
        for xi, b, value in ends:
            bottom[xi, pl.ds(b, 1), :] = value
        return 0

    lax.fori_loop(0, bins // 4, group, 0)


def micro_kernel(nx, xs, slots, merge, *refs):
    if merge:
        scal, index, settled, carry, table, sat_ref, mask_ref, inner, out, grown, change = refs
    else:
        scal, index, settled, carry, table, sat_ref, mask_ref, out, grown, change = refs
    bins = settled.shape[0]
    drops = grown.shape[0]
    aero = bins - drops
    cells = grown.shape[1]
    blocks = cells // len(xs)
    at_growth = bins + blocks * bins
    at_threshold = at_growth + drops
    at_rate = at_threshold + aero

    def spans(v):
        x, q = xs[v // blocks], v % blocks
        return pl.ds(q * SUB * nx + x, SUB, stride=nx)

    sat = [sat_ref[spans(v), :] for v in range(cells)]

    def full(b):
        values = []
        decay = table[b, 3]
        for v in range(cells):
            xi, q = v // blocks, v % blocks
            values.append(
                settled[b, v]
                + (decay * scal[bins + q * bins + b]) * carry[xi, pl.ds(b, 1), :]
            )
        return values

    def put(b, v, value):
        if merge:
            out[b, spans(v), :] = value
        else:
            out[b, v] = value

    zero = jnp.zeros((SUB, LANES), jnp.float32)

    def activate(j, gained):
        mass = full(drops + j)
        fresh = []
        for v in range(cells):
            active = jnp.maximum(sat[v] - scal[at_threshold + j], 0.0) * mass[v]
            put(drops + j, v, mass[v] - active)
            fresh.append(gained[v] + active)
        return tuple(fresh)

    gained = lax.fori_loop(0, aero, activate, (zero,) * cells)

    def condense(b, state):
        current, below = state
        after = full(b + 1)
        flux = []
        for v in range(cells):
            face = scal[at_growth + b] * sat[v]
            flux.append(jnp.maximum(face, 0.0) * current[v] + jnp.minimum(face, 0.0) * after[v])
            grown[b, v] = current[v] + below[v] - flux[v]
            change[b, v] = zero
        return tuple(after), tuple(flux)

    current, below = lax.fori_loop(
        0, drops - 1, condense, (tuple(full(0)), (zero,) * cells)
    )
    for v in range(cells):
        grown[drops - 1, v] = current[v] + below[v]
        change[drops - 1, v] = zero
        grown[0, v] = grown[0, v] + gained[v]

    def collide(i, _):
        mine = grown[i]
        loss = jnp.zeros_like(mine)
        for m in range(slots):
            pair = i * slots + m
            rate = (mine * scal[at_rate + pair]) * grown[index[pair]]
            loss = loss + rate
            goal = index[drops * slots + pair]
            change[goal] = change[goal] + rate
        change[i] = change[i] - loss
        return 0

    lax.fori_loop(0, drops, collide, 0)

    mask = [mask_ref[spans(v), :].astype(jnp.float32) for v in range(cells)]

    def finish(b, _):
        for v in range(cells):
            put(b, v, grown[b, v] + mask[v] * change[b, v])
        return 0

    lax.fori_loop(0, drops, finish, 0)

    if merge:
        others = [x for x in range(nx) if x not in xs]

        def fill(b, _):
            for xi, x in enumerate(others):
                for q in range(blocks):
                    out[b, pl.ds(q * SUB * nx + x, SUB, stride=nx), :] = inner[b, xi * blocks + q]
            return 0

        lax.fori_loop(0, bins, fill, 0)


VMEM = pl.BlockSpec(memory_space=pltpu.VMEM)
SMEM = pl.BlockSpec(memory_space=pltpu.SMEM)
PARAMS = pltpu.CompilerParams(vmem_limit_bytes=24 * 1024 * 1024)


def cost(flops, bytes_accessed):
    return pl.CostEstimate(flops=flops, bytes_accessed=bytes_accessed, transcendentals=0)


def shift_up(value, axis):
    count = lax.axis_size(axis)
    return lax.ppermute(value, axis, [(i, (i + 1) % count) for i in range(count)])


def shift_down(value, axis):
    count = lax.axis_size(axis)
    return lax.ppermute(value, axis, [((i + 1) % count, i) for i in range(count)])


def shards(
    field,
    courant_x,
    courant_y,
    supersat,
    cloud_mask,
    fall_speed,
    growth,
    activation_threshold,
    kernel_rate,
    partner,
    target,
):
    bins, depth, nx, ny = field.shape
    drops, slots = partner.shape
    f32 = jnp.float32
    blocks = depth // SUB
    flat = field.reshape(bins, depth * nx, ny)
    cx, cy, sat, mask = (
        a.reshape(depth * nx, ny) for a in (courant_x, courant_y, supersat, cloud_mask)
    )

    groups = bins // GROUP
    face = jax.ShapeDtypeStruct((bins, depth, ny), f32)
    to_right, to_left = pl.pallas_call(
        functools.partial(pack_x_kernel, nx),
        out_shape=(face, face),
        in_specs=[VMEM],
        out_specs=(VMEM, VMEM),
        compiler_params=PARAMS,
        cost_estimate=cost(1 << 20, 6 << 20),
        name="pack_x",
    )(flat)
    x_left = shift_up(to_right, "gx")
    x_right = shift_down(to_left, "gx")
    cy, cx_last, to_right, to_left = lax.optimization_barrier((cy, courant_x, to_right, to_left))
    cx_left = shift_up(cx_last[:, nx - 1, :], "gx")

    y_to_right, y_to_left = pl.pallas_call(
        functools.partial(pack_y_kernel, nx),
        out_shape=(
            jax.ShapeDtypeStruct((groups + 1, SUB, LANES), f32),
            jax.ShapeDtypeStruct((groups, SUB, LANES), f32),
        ),
        in_specs=[VMEM, VMEM],
        out_specs=(VMEM, VMEM),
        compiler_params=PARAMS,
        cost_estimate=cost(1 << 22, 1 << 22),
        name="pack_y",
    )(flat, cy)
    y_left = shift_up(y_to_right, "gy")
    y_right = shift_down(y_to_left, "gy")

    ratio = fall_speed / (1.0 + fall_speed)
    log_ratio = jnp.log(ratio)
    sub = jnp.arange(SUB, dtype=f32)
    power = jnp.stack([jnp.full((SUB,), 1.0, f32), jnp.full((SUB,), 2.0, f32), jnp.full((SUB,), 4.0, f32), SUB - sub])
    keep = jnp.stack([sub < SUB - 1, sub < SUB - 2, sub < SUB - 4, sub < SUB])
    table = jnp.where(keep, jnp.exp(log_ratio[:, None, None] * power), 0.0)
    table = jnp.broadcast_to(table[..., None], (bins, 4, SUB, LANES))
    step = jnp.exp(log_ratio[None, :] * (SUB * jnp.arange(blocks - 1, -1, -1, dtype=f32))[:, None])
    scal = jnp.concatenate(
        [
            1.0 / (1.0 + fall_speed),
            step.reshape(-1),
            growth,
            jnp.zeros((1,), f32),
            activation_threshold,
            kernel_rate.reshape(-1),
        ]
    )
    index = jnp.concatenate([partner.reshape(-1), target.reshape(-1)])

    inner_x = tuple(range(1, nx - 1))
    edge_x = (0, nx - 1)

    def settle_shapes(xs):
        return (
            jax.ShapeDtypeStruct((bins, len(xs) * blocks, SUB, LANES), f32),
            jax.ShapeDtypeStruct((len(xs), bins, LANES), f32),
        )

    count = lax.axis_size("gz")
    whole = jnp.exp(log_ratio * depth)[None, :, None]

    def inflow(bottom):
        carry = jnp.zeros_like(bottom)
        for hop in range(count - 1):
            sent = bottom if hop == 0 else bottom + whole * carry
            carry = lax.ppermute(sent, "gz", [(i + 1, i) for i in range(count - 1)])
        return carry

    def micro_part(xs, settled, carry, inner):
        cells = len(xs) * blocks
        args = [scal, index, settled, carry, table, sat, mask] + list(inner)
        if inner:
            out = jax.ShapeDtypeStruct((bins, depth * nx, ny), f32)
        else:
            out = jax.ShapeDtypeStruct((bins, cells, SUB, LANES), f32)
        return pl.pallas_call(
            functools.partial(micro_kernel, nx, xs, slots, bool(inner)),
            out_shape=out,
            in_specs=[SMEM, SMEM] + [VMEM] * (len(args) - 2),
            out_specs=VMEM,
            scratch_shapes=[
                pltpu.VMEM((drops, cells, SUB, LANES), f32),
                pltpu.VMEM((drops, cells, SUB, LANES), f32),
            ],
            compiler_params=PARAMS,
            cost_estimate=cost(1 << 24, 8 << 20),
            name="micro_edge" if inner else "micro_inner",
        )(*args)

    settled, bottom, part, part_bottom = pl.pallas_call(
        functools.partial(settle_kernel, nx, (inner_x, edge_x)),
        out_shape=settle_shapes(inner_x) + settle_shapes(edge_x),
        in_specs=[SMEM] + [VMEM] * 6,
        out_specs=(VMEM,) * 4,
        compiler_params=PARAMS,
        cost_estimate=cost(1 << 24, 16 << 20),
        name="settle_all",
    )(scal, flat, cx, cy, y_left, y_right, table)
    inner_carry = inflow(bottom)
    edge_settled, edge_bottom = pl.pallas_call(
        functools.partial(edge_kernel, nx),
        out_shape=settle_shapes(edge_x),
        in_specs=[SMEM] + [VMEM] * 8,
        out_specs=(VMEM,) * 2,
        compiler_params=PARAMS,
        cost_estimate=cost(1 << 23, 8 << 20),
        name="settle_edge",
    )(scal, part, part_bottom, cx, table, cx_left, to_left, x_left, x_right)
    settled, edge_bottom = lax.optimization_barrier((settled, edge_bottom))
    edge_carry = inflow(edge_bottom)
    inner = micro_part(inner_x, settled, inner_carry, ())
    out = micro_part(edge_x, edge_settled, edge_carry, (inner,))
    return out.reshape(field.shape)


def solution(mesh):
    cells = P("gz", "gx", "gy")
    return jax.shard_map(
        shards,
        mesh=mesh,
        in_specs=(P(None, "gz", "gx", "gy"), cells, cells, cells, cells) + (P(),) * 6,
        out_specs=P(None, "gz", "gx", "gy"),
        check_vma=False,
    )
```

```python
import functools

import jax
import jax.numpy as jnp
from jax import lax
from jax.experimental import pallas as pl
from jax.experimental.pallas import tpu as pltpu
from jax.sharding import PartitionSpec as P

LANES = 128
SUB = 8
GROUP = 8
WRITES = 4


def roll_to(value, source, dest):
    shift = (dest - source) % LANES
    return value if shift == 0 else pltpu.roll(value, shift, 1)


def lane_of(at):
    return 2 * (at % (LANES // 2)) + at // (LANES // 2)


def pack_x_kernel(nx, field_ref, right_ref, left_ref):
    bins, rows, _ = field_ref.shape

    def group(g, _):
        for k in range(GROUP):
            b = g * GROUP + k
            for q in range(rows // (SUB * nx)):
                start = q * SUB * nx
                zrows = pl.ds(q * SUB, SUB)
                right_ref[b, zrows, :] = field_ref[b, pl.ds(start + nx - 1, SUB, stride=nx), :]
                left_ref[b, zrows, :] = field_ref[b, pl.ds(start, SUB, stride=nx), :]
        return 0

    lax.fori_loop(0, bins // GROUP, group, 0)


def pack_y_kernel(nx, field_ref, cour_ref, right_ref, left_ref):
    bins, rows, _ = field_ref.shape
    per_bin = rows // SUB
    blocks = rows // (SUB * nx)
    lane = lax.broadcasted_iota(jnp.int32, (SUB, LANES), 1)

    def one(load, offset, packed):
        for x in range(nx):
            for q in range(blocks):
                at = lane_of(offset + x * blocks + q)
                under = (at - 1) % LANES
                value = load(pl.ds(q * SUB * nx + x, SUB, stride=nx))
                packed = (
                    jnp.where(lane == at, roll_to(value, LANES - 1, at), packed[0]),
                    jnp.where(lane == under, roll_to(value, 0, under), packed[1]),
                )
        return packed

    zero = jnp.zeros((SUB, LANES), jnp.float32)

    def group(g, _):
        packed = (zero, zero)
        for k in range(GROUP):
            packed = one(lambda r: field_ref[g * GROUP + k, r, :], k * per_bin, packed)
        right_ref[g] = packed[0]
        left_ref[g] = packed[1]
        return 0

    lax.fori_loop(0, bins // GROUP, group, 0)
    right_ref[bins // GROUP] = one(lambda r: cour_ref[r, :], 0, (zero, zero))[0]


def scan_levels(value, table, b):
    value = value + table[b, 0] * pltpu.roll(value, SUB - 1, 0)
    value = value + table[b, 1] * pltpu.roll(value, SUB - 2, 0)
    return value + table[b, 2] * pltpu.roll(value, SUB - 4, 0)


def settle_kernel(nx, sets, *refs):
    scal, field, cx, cy, yl, yr, table = refs[:7]
    outs = refs[7:]
    bins, rows, _ = field.shape
    blocks = rows // (SUB * nx)
    per_bin = nx * blocks
    lane = lax.broadcasted_iota(jnp.int32, (SUB, LANES), 1)
    first, last = lane == 0, lane == LANES - 1
    even = lane % 2 == 0
    place = {x: (n, xi) for n, xs in enumerate(sets) for xi, x in enumerate(xs)}
    half = GROUP // 2
    for q in reversed(range(blocks)):
        spans = [pl.ds(q * SUB * nx + x, SUB, stride=nx) for x in range(nx)]
        c_all = [cx[spans[x], :] for x in range(nx)]
        stay, from_up, from_down = [], [], []
        for x in range(nx):
            y_here = cy[spans[x], :]
            edge = roll_to(yl[bins // GROUP], lane_of(x * blocks + q), 0)
            y_left = jnp.where(first, edge, pltpu.roll(y_here, 1, 1))
            kept = (
                1.0
                - jnp.maximum(c_all[x], 0.0)
                - jnp.maximum(y_here, 0.0)
                + jnp.minimum(y_left, 0.0)
            )
            if x > 0:
                kept = kept + jnp.minimum(c_all[x - 1], 0.0)
            stay.append(kept)
            from_up.append(-jnp.minimum(y_here, 0.0))
            from_down.append(jnp.maximum(y_left, 0.0))
        enters = [jnp.maximum(c, 0.0) for c in c_all]
        backs = [-jnp.minimum(c, 0.0) for c in c_all]

        def group(g, _):
            packs = (jnp.where(even, yl[g], yr[g]), jnp.where(even, yr[g], yl[g]))
            for part in range(2):
                falls = []
                for k in range(part * half, (part + 1) * half):
                    b = g * GROUP + k
                    row = [field[b, spans[x], :] for x in range(nx)]
                    for x in range(nx):
                        n, xi = place[x]
                        at = k * per_bin + x * blocks + q
                        halo = roll_to(packs[at // (LANES // 2)], lane_of(at), 0)
                        down = jnp.where(first, halo, pltpu.roll(row[x], 1, 1))
                        up = jnp.where(last, halo, pltpu.roll(row[x], LANES - 1, 1))
                        moved = stay[x] * row[x] + from_up[x] * up + from_down[x] * down
                        if x > 0:
                            moved = moved + enters[x - 1] * row[x - 1]
                        if x < nx - 1:
                            moved = moved + backs[x] * row[x + 1]
                        fall = scan_levels(moved * scal[b], table, b)
                        if q < blocks - 1:
                            above = outs[2 * n][b, xi * blocks + q + 1, pl.ds(0, 1), :]
                            fall = fall + table[b, 3] * above
                        falls.append((n, xi, b, fall))
                for n, xi, b, fall in falls:
                    outs[2 * n][b, xi * blocks + q] = fall
                    if q == 0:
                        outs[2 * n + 1][xi, pl.ds(b, 1), :] = fall[0:1, :]
            return 0

        lax.fori_loop(0, bins // GROUP, group, 0)


def edge_kernel(nx, *refs):
    scal, part, part_bottom, cx, table, cl, own, xl, xr, out, bottom = refs
    bins, cells = part.shape[:2]
    blocks = cells // 2
    leaves = [jnp.minimum(cl[pl.ds(q * SUB, SUB), :], 0.0) for q in range(blocks)]
    enters = [jnp.maximum(cl[pl.ds(q * SUB, SUB), :], 0.0) for q in range(blocks)]
    backs = [
        -jnp.minimum(cx[pl.ds(q * SUB * nx + nx - 1, SUB, stride=nx), :], 0.0)
        for q in range(blocks)
    ]

    def group(g, _):
        values, ends = [], []
        for k in range(4):
            b = g * 4 + k
            for xi in range(2):
                above = None
                for q in reversed(range(blocks)):
                    zrows = pl.ds(q * SUB, SUB)
                    if xi == 0:
                        flux = enters[q] * xl[b, zrows, :] + leaves[q] * own[b, zrows, :]
                    else:
                        flux = backs[q] * xr[b, zrows, :]
                    fall = scan_levels(flux * scal[b], table, b)
                    if above is not None:
                        fall = fall + table[b, 3] * above
                    above = fall[0:1, :]
                    values.append((b, xi * blocks + q, fall + part[b, xi * blocks + q]))
                ends.append((xi, b, above + part_bottom[xi, pl.ds(b, 1), :]))
        for b, v, value in values:
            out[b, v] = value
        for xi, b, value in ends:
            bottom[xi, pl.ds(b, 1), :] = value
        return 0

    lax.fori_loop(0, bins // 4, group, 0)


def micro_kernel(nx, xs, slots, merge, *refs):
    if merge:
        scal, index, settled, carry, table, sat_ref, mask_ref, inner, final = refs[:9]
        grown, change, out, sems = refs[9:]
    else:
        scal, index, settled, carry, table, sat_ref, mask_ref, out, grown, change = refs
    bins = settled.shape[0]
    drops = grown.shape[0]
    aero = bins - drops
    cells = grown.shape[1]
    blocks = cells // len(xs)
    at_growth = bins + blocks * bins
    at_threshold = at_growth + drops
    at_rate = at_threshold + aero

    def spans(v):
        x, q = xs[v // blocks], v % blocks
        return pl.ds(q * SUB * nx + x, SUB, stride=nx)

    sat = [sat_ref[spans(v), :] for v in range(cells)]

    def full(b):
        values = []
        decay = table[b, 3]
        for v in range(cells):
            xi, q = v // blocks, v % blocks
            values.append(
                settled[b, v]
                + (decay * scal[bins + q * bins + b]) * carry[xi, pl.ds(b, 1), :]
            )
        return values

    def put(b, v, value):
        if merge:
            out[b, spans(v), :] = value
        else:
            out[b, v] = value

    zero = jnp.zeros((SUB, LANES), jnp.float32)

    def activate(j, gained):
        mass = full(drops + j)
        fresh = []
        for v in range(cells):
            active = jnp.maximum(sat[v] - scal[at_threshold + j], 0.0) * mass[v]
            put(drops + j, v, mass[v] - active)
            fresh.append(gained[v] + active)
        return tuple(fresh)

    def fill(b, _):
        others = [x for x in range(nx) if x not in xs]
        for xi, x in enumerate(others):
            for q in range(blocks):
                out[b, pl.ds(q * SUB * nx + x, SUB, stride=nx), :] = inner[b, xi * blocks + q]
        return 0

    copies = []

    def send(begin, size):
        part = pl.ds(begin, size)
        copy = pltpu.make_async_copy(out.at[part], final.at[part], sems.at[len(copies)])
        copy.start()
        copies.append(copy)

    gained = lax.fori_loop(0, aero, activate, (zero,) * cells)
    if merge:
        lax.fori_loop(drops, bins, fill, 0)
        send(drops, aero)

    def condense(b, state):
        current, below = state
        after = full(b + 1)
        flux = []
        for v in range(cells):
            face = scal[at_growth + b] * sat[v]
            flux.append(jnp.maximum(face, 0.0) * current[v] + jnp.minimum(face, 0.0) * after[v])
            grown[b, v] = current[v] + below[v] - flux[v]
            change[b, v] = zero
        return tuple(after), tuple(flux)

    current, below = lax.fori_loop(
        0, drops - 1, condense, (tuple(full(0)), (zero,) * cells)
    )
    for v in range(cells):
        grown[drops - 1, v] = current[v] + below[v]
        change[drops - 1, v] = zero
        grown[0, v] = grown[0, v] + gained[v]

    def collide(i, _):
        mine = grown[i]
        loss = jnp.zeros_like(mine)
        for m in range(slots):
            pair = i * slots + m
            rate = (mine * scal[at_rate + pair]) * grown[index[pair]]
            loss = loss + rate
            goal = index[drops * slots + pair]
            change[goal] = change[goal] + rate
        change[i] = change[i] - loss
        return 0

    lax.fori_loop(0, drops, collide, 0)

    mask = [mask_ref[spans(v), :].astype(jnp.float32) for v in range(cells)]

    def finish(b, _):
        for v in range(cells):
            put(b, v, grown[b, v] + mask[v] * change[b, v])
        return 0

    if merge:
        lax.fori_loop(0, drops, fill, 0)
        size = drops // WRITES
        for n in range(WRITES):
            begin = n * size
            end = begin + size if n < WRITES - 1 else drops
            lax.fori_loop(begin, end, finish, 0)
            send(begin, end - begin)
        for copy in copies:
            copy.wait()
    else:
        lax.fori_loop(0, drops, finish, 0)


VMEM = pl.BlockSpec(memory_space=pltpu.VMEM)
SMEM = pl.BlockSpec(memory_space=pltpu.SMEM)
PARAMS = pltpu.CompilerParams(vmem_limit_bytes=24 * 1024 * 1024)


def cost(flops, bytes_accessed):
    return pl.CostEstimate(flops=flops, bytes_accessed=bytes_accessed, transcendentals=0)


def shift_up(value, axis):
    count = lax.axis_size(axis)
    return lax.ppermute(value, axis, [(i, (i + 1) % count) for i in range(count)])


def shift_down(value, axis):
    count = lax.axis_size(axis)
    return lax.ppermute(value, axis, [((i + 1) % count, i) for i in range(count)])


def shards(
    field,
    courant_x,
    courant_y,
    supersat,
    cloud_mask,
    fall_speed,
    growth,
    activation_threshold,
    kernel_rate,
    partner,
    target,
):
    bins, depth, nx, ny = field.shape
    drops, slots = partner.shape
    f32 = jnp.float32
    blocks = depth // SUB
    flat = field.reshape(bins, depth * nx, ny)
    cx, cy, sat, mask = (
        a.reshape(depth * nx, ny) for a in (courant_x, courant_y, supersat, cloud_mask)
    )

    groups = bins // GROUP
    face = jax.ShapeDtypeStruct((bins, depth, ny), f32)
    to_right, to_left = pl.pallas_call(
        functools.partial(pack_x_kernel, nx),
        out_shape=(face, face),
        in_specs=[VMEM],
        out_specs=(VMEM, VMEM),
        compiler_params=PARAMS,
        cost_estimate=cost(1 << 20, 6 << 20),
        name="pack_x",
    )(flat)
    x_left = shift_up(to_right, "gx")
    x_right = shift_down(to_left, "gx")
    cy, cx_last, to_right, to_left = lax.optimization_barrier((cy, courant_x, to_right, to_left))
    cx_left = shift_up(cx_last[:, nx - 1, :], "gx")

    y_to_right, y_to_left = pl.pallas_call(
        functools.partial(pack_y_kernel, nx),
        out_shape=(
            jax.ShapeDtypeStruct((groups + 1, SUB, LANES), f32),
            jax.ShapeDtypeStruct((groups, SUB, LANES), f32),
        ),
        in_specs=[VMEM, VMEM],
        out_specs=(VMEM, VMEM),
        compiler_params=PARAMS,
        cost_estimate=cost(1 << 22, 1 << 22),
        name="pack_y",
    )(flat, cy)
    y_left = shift_up(y_to_right, "gy")
    y_right = shift_down(y_to_left, "gy")

    ratio = fall_speed / (1.0 + fall_speed)
    log_ratio = jnp.log(ratio)
    sub = jnp.arange(SUB, dtype=f32)
    power = jnp.stack([jnp.full((SUB,), 1.0, f32), jnp.full((SUB,), 2.0, f32), jnp.full((SUB,), 4.0, f32), SUB - sub])
    keep = jnp.stack([sub < SUB - 1, sub < SUB - 2, sub < SUB - 4, sub < SUB])
    table = jnp.where(keep, jnp.exp(log_ratio[:, None, None] * power), 0.0)
    table = jnp.broadcast_to(table[..., None], (bins, 4, SUB, LANES))
    step = jnp.exp(log_ratio[None, :] * (SUB * jnp.arange(blocks - 1, -1, -1, dtype=f32))[:, None])
    scal = jnp.concatenate(
        [
            1.0 / (1.0 + fall_speed),
            step.reshape(-1),
            growth,
            jnp.zeros((1,), f32),
            activation_threshold,
            kernel_rate.reshape(-1),
        ]
    )
    index = jnp.concatenate([partner.reshape(-1), target.reshape(-1)])

    inner_x = tuple(range(1, nx - 1))
    edge_x = (0, nx - 1)

    def settle_shapes(xs):
        return (
            jax.ShapeDtypeStruct((bins, len(xs) * blocks, SUB, LANES), f32),
            jax.ShapeDtypeStruct((len(xs), bins, LANES), f32),
        )

    count = lax.axis_size("gz")
    whole = jnp.exp(log_ratio * depth)[None, :, None]

    def inflow(bottom):
        carry = jnp.zeros_like(bottom)
        for hop in range(count - 1):
            sent = bottom if hop == 0 else bottom + whole * carry
            carry = lax.ppermute(sent, "gz", [(i + 1, i) for i in range(count - 1)])
        return carry

    def micro_part(xs, settled, carry, inner):
        cells = len(xs) * blocks
        args = [scal, index, settled, carry, table, sat, mask] + list(inner)
        if inner:
            out = jax.ShapeDtypeStruct((bins, depth * nx, ny), f32)
        else:
            out = jax.ShapeDtypeStruct((bins, cells, SUB, LANES), f32)
        return pl.pallas_call(
            functools.partial(micro_kernel, nx, xs, slots, bool(inner)),
            out_shape=out,
            in_specs=[SMEM, SMEM] + [VMEM] * (len(args) - 2),
            out_specs=pl.BlockSpec(memory_space=pl.ANY) if inner else VMEM,
            scratch_shapes=[
                pltpu.VMEM((drops, cells, SUB, LANES), f32),
                pltpu.VMEM((drops, cells, SUB, LANES), f32),
            ]
            + ([pltpu.VMEM(out.shape, f32), pltpu.SemaphoreType.DMA((WRITES + 1,))] if inner else []),
            compiler_params=PARAMS,
            cost_estimate=cost(1 << 24, 8 << 20),
            name="micro_edge" if inner else "micro_inner",
        )(*args)

    settled, bottom, part, part_bottom = pl.pallas_call(
        functools.partial(settle_kernel, nx, (inner_x, edge_x)),
        out_shape=settle_shapes(inner_x) + settle_shapes(edge_x),
        in_specs=[SMEM] + [VMEM] * 6,
        out_specs=(VMEM,) * 4,
        compiler_params=PARAMS,
        cost_estimate=cost(1 << 24, 16 << 20),
        name="settle_all",
    )(scal, flat, cx, cy, y_left, y_right, table)
    inner_carry = inflow(bottom)
    edge_settled, edge_bottom = pl.pallas_call(
        functools.partial(edge_kernel, nx),
        out_shape=settle_shapes(edge_x),
        in_specs=[SMEM] + [VMEM] * 8,
        out_specs=(VMEM,) * 2,
        compiler_params=PARAMS,
        cost_estimate=cost(1 << 23, 8 << 20),
        name="settle_edge",
    )(scal, part, part_bottom, cx, table, cx_left, to_left, x_left, x_right)
    settled, edge_bottom = lax.optimization_barrier((settled, edge_bottom))
    edge_carry = inflow(edge_bottom)
    inner = micro_part(inner_x, settled, inner_carry, ())
    out = micro_part(edge_x, edge_settled, edge_carry, (inner,))
    return out.reshape(field.shape)


def solution(mesh):
    cells = P("gz", "gx", "gy")
    return jax.shard_map(
        shards,
        mesh=mesh,
        in_specs=(P(None, "gz", "gx", "gy"), cells, cells, cells, cells) + (P(),) * 6,
        out_specs=P(None, "gz", "gx", "gy"),
        check_vma=False,
    )
```

```python
import functools

import jax
import jax.numpy as jnp
from jax import lax
from jax.experimental import pallas as pl
from jax.experimental.pallas import tpu as pltpu
from jax.sharding import PartitionSpec as P

LANES = 128
SUB = 8
GROUP = 8
WRITES = 4


def roll_to(value, source, dest):
    shift = (dest - source) % LANES
    return value if shift == 0 else pltpu.roll(value, shift, 1)


def lane_of(at):
    return 2 * (at % (LANES // 2)) + at // (LANES // 2)


def pack_x_kernel(nx, field_ref, right_ref, left_ref):
    bins, rows, _ = field_ref.shape

    def group(g, _):
        for k in range(GROUP):
            b = g * GROUP + k
            for q in range(rows // (SUB * nx)):
                start = q * SUB * nx
                zrows = pl.ds(q * SUB, SUB)
                right_ref[b, zrows, :] = field_ref[b, pl.ds(start + nx - 1, SUB, stride=nx), :]
                left_ref[b, zrows, :] = field_ref[b, pl.ds(start, SUB, stride=nx), :]
        return 0

    lax.fori_loop(0, bins // GROUP, group, 0)


def pack_y_kernel(nx, field_ref, cour_ref, right_ref, left_ref):
    bins, rows, _ = field_ref.shape
    per_bin = rows // SUB
    blocks = rows // (SUB * nx)
    lane = lax.broadcasted_iota(jnp.int32, (SUB, LANES), 1)

    def one(load, offset, packed):
        for x in range(nx):
            for q in range(blocks):
                at = lane_of(offset + x * blocks + q)
                under = (at - 1) % LANES
                value = load(pl.ds(q * SUB * nx + x, SUB, stride=nx))
                packed = (
                    jnp.where(lane == at, roll_to(value, LANES - 1, at), packed[0]),
                    jnp.where(lane == under, roll_to(value, 0, under), packed[1]),
                )
        return packed

    zero = jnp.zeros((SUB, LANES), jnp.float32)

    def group(g, _):
        packed = (zero, zero)
        for k in range(GROUP):
            packed = one(lambda r: field_ref[g * GROUP + k, r, :], k * per_bin, packed)
        right_ref[g] = packed[0]
        left_ref[g] = packed[1]
        return 0

    lax.fori_loop(0, bins // GROUP, group, 0)
    right_ref[bins // GROUP] = one(lambda r: cour_ref[r, :], 0, (zero, zero))[0]


def scan_levels(value, table, b):
    value = value + table[b, 0] * pltpu.roll(value, SUB - 1, 0)
    value = value + table[b, 1] * pltpu.roll(value, SUB - 2, 0)
    return value + table[b, 2] * pltpu.roll(value, SUB - 4, 0)


def settle_kernel(nx, sets, *refs):
    scal, field, cx, cy, yl, yr, table = refs[:7]
    outs = refs[7:]
    bins, rows, _ = field.shape
    blocks = rows // (SUB * nx)
    per_bin = nx * blocks
    lane = lax.broadcasted_iota(jnp.int32, (SUB, LANES), 1)
    first, last = lane == 0, lane == LANES - 1
    even = lane % 2 == 0
    place = {x: (n, xi) for n, xs in enumerate(sets) for xi, x in enumerate(xs)}
    half = GROUP // 2
    for q in reversed(range(blocks)):
        spans = [pl.ds(q * SUB * nx + x, SUB, stride=nx) for x in range(nx)]
        c_all = [cx[spans[x], :] for x in range(nx)]
        stay, from_up, from_down = [], [], []
        for x in range(nx):
            y_here = cy[spans[x], :]
            edge = roll_to(yl[bins // GROUP], lane_of(x * blocks + q), 0)
            y_left = jnp.where(first, edge, pltpu.roll(y_here, 1, 1))
            kept = (
                1.0
                - jnp.maximum(c_all[x], 0.0)
                - jnp.maximum(y_here, 0.0)
                + jnp.minimum(y_left, 0.0)
            )
            if x > 0:
                kept = kept + jnp.minimum(c_all[x - 1], 0.0)
            stay.append(kept)
            from_up.append(-jnp.minimum(y_here, 0.0))
            from_down.append(jnp.maximum(y_left, 0.0))
        enters = [jnp.maximum(c, 0.0) for c in c_all]
        backs = [-jnp.minimum(c, 0.0) for c in c_all]

        def group(g, _):
            packs = (jnp.where(even, yl[g], yr[g]), jnp.where(even, yr[g], yl[g]))
            for part in range(2):
                falls = []
                for k in range(part * half, (part + 1) * half):
                    b = g * GROUP + k
                    row = [field[b, spans[x], :] for x in range(nx)]
                    for x in range(nx):
                        n, xi = place[x]
                        at = k * per_bin + x * blocks + q
                        halo = roll_to(packs[at // (LANES // 2)], lane_of(at), 0)
                        down = jnp.where(first, halo, pltpu.roll(row[x], 1, 1))
                        up = jnp.where(last, halo, pltpu.roll(row[x], LANES - 1, 1))
                        moved = stay[x] * row[x] + from_up[x] * up + from_down[x] * down
                        if x > 0:
                            moved = moved + enters[x - 1] * row[x - 1]
                        if x < nx - 1:
                            moved = moved + backs[x] * row[x + 1]
                        fall = scan_levels(moved * scal[b], table, b)
                        if q < blocks - 1:
                            above = outs[2 * n][b, xi * blocks + q + 1, pl.ds(0, 1), :]
                            fall = fall + table[b, 3] * above
                        falls.append((n, xi, b, fall))
                for n, xi, b, fall in falls:
                    outs[2 * n][b, xi * blocks + q] = fall
                    if q == 0:
                        outs[2 * n + 1][xi, pl.ds(b, 1), :] = fall[0:1, :]
            return 0

        lax.fori_loop(0, bins // GROUP, group, 0)


def edge_kernel(nx, *refs):
    scal, part, part_bottom, cx, table, cl, own, xl, xr, out, bottom = refs
    bins, cells = part.shape[:2]
    blocks = cells // 2
    leaves = [jnp.minimum(cl[pl.ds(q * SUB, SUB), :], 0.0) for q in range(blocks)]
    enters = [jnp.maximum(cl[pl.ds(q * SUB, SUB), :], 0.0) for q in range(blocks)]
    backs = [
        -jnp.minimum(cx[pl.ds(q * SUB * nx + nx - 1, SUB, stride=nx), :], 0.0)
        for q in range(blocks)
    ]

    def group(g, _):
        values, ends = [], []
        for k in range(4):
            b = g * 4 + k
            for xi in range(2):
                above = None
                for q in reversed(range(blocks)):
                    zrows = pl.ds(q * SUB, SUB)
                    if xi == 0:
                        flux = enters[q] * xl[b, zrows, :] + leaves[q] * own[b, zrows, :]
                    else:
                        flux = backs[q] * xr[b, zrows, :]
                    fall = scan_levels(flux * scal[b], table, b)
                    if above is not None:
                        fall = fall + table[b, 3] * above
                    above = fall[0:1, :]
                    values.append((b, xi * blocks + q, fall + part[b, xi * blocks + q]))
                ends.append((xi, b, above + part_bottom[xi, pl.ds(b, 1), :]))
        for b, v, value in values:
            out[b, v] = value
        for xi, b, value in ends:
            bottom[xi, pl.ds(b, 1), :] = value
        return 0

    lax.fori_loop(0, bins // 4, group, 0)


def micro_kernel(nx, xs, slots, merge, *refs):
    if merge:
        scal, index, settled, carry, table, sat_ref, mask_ref, inner, final = refs[:9]
        grown, change, out, sems = refs[9:]
    else:
        scal, index, settled, carry, table, sat_ref, mask_ref, out, grown, change = refs
    bins = settled.shape[0]
    drops = grown.shape[0]
    aero = bins - drops
    cells = grown.shape[1]
    blocks = cells // len(xs)
    at_growth = bins + blocks * bins
    at_threshold = at_growth + drops
    at_rate = at_threshold + aero

    def spans(v):
        x, q = xs[v // blocks], v % blocks
        return pl.ds(q * SUB * nx + x, SUB, stride=nx)

    sat = [sat_ref[spans(v), :] for v in range(cells)]

    def full(b):
        values = []
        decay = table[b, 3]
        for v in range(cells):
            xi, q = v // blocks, v % blocks
            values.append(
                settled[b, v]
                + (decay * scal[bins + q * bins + b]) * carry[xi, pl.ds(b, 1), :]
            )
        return values

    def put(b, v, value):
        if merge:
            out[b, spans(v), :] = value
        else:
            out[b, v] = value

    zero = jnp.zeros((SUB, LANES), jnp.float32)

    def activate(j, gained):
        mass = full(drops + j)
        fresh = []
        for v in range(cells):
            active = jnp.maximum(sat[v] - scal[at_threshold + j], 0.0) * mass[v]
            put(drops + j, v, mass[v] - active)
            fresh.append(gained[v] + active)
        return tuple(fresh)

    def fill(b, _):
        others = [x for x in range(nx) if x not in xs]
        for xi, x in enumerate(others):
            for q in range(blocks):
                out[b, pl.ds(q * SUB * nx + x, SUB, stride=nx), :] = inner[b, xi * blocks + q]
        return 0

    copies = []

    def send(begin, size):
        part = pl.ds(begin, size)
        copy = pltpu.make_async_copy(out.at[part], final.at[part], sems.at[len(copies)])
        copy.start()
        copies.append(copy)

    gained = lax.fori_loop(0, aero, activate, (zero,) * cells)
    if merge:
        lax.fori_loop(drops, bins, fill, 0, unroll=4)
        send(drops, aero)

    def condense(b, state):
        current, below = state
        after = full(b + 1)
        flux = []
        for v in range(cells):
            face = scal[at_growth + b] * sat[v]
            flux.append(jnp.maximum(face, 0.0) * current[v] + jnp.minimum(face, 0.0) * after[v])
            grown[b, v] = current[v] + below[v] - flux[v]
            change[b, v] = zero
        return tuple(after), tuple(flux)

    current, below = lax.fori_loop(
        0, drops - 1, condense, (tuple(full(0)), (zero,) * cells)
    )
    for v in range(cells):
        grown[drops - 1, v] = current[v] + below[v]
        change[drops - 1, v] = zero
        grown[0, v] = grown[0, v] + gained[v]

    def collide(i, _):
        mine = grown[i]
        loss = jnp.zeros_like(mine)
        for m in range(slots):
            pair = i * slots + m
            rate = (mine * scal[at_rate + pair]) * grown[index[pair]]
            loss = loss + rate
            goal = index[drops * slots + pair]
            change[goal] = change[goal] + rate
        change[i] = change[i] - loss
        return 0

    lax.fori_loop(0, drops, collide, 0, unroll=2)

    mask = [mask_ref[spans(v), :].astype(jnp.float32) for v in range(cells)]

    def finish(b, _):
        for v in range(cells):
            put(b, v, grown[b, v] + mask[v] * change[b, v])
        return 0

    if merge:
        lax.fori_loop(0, drops, fill, 0, unroll=4)
        size = drops // WRITES
        for n in range(WRITES):
            begin = n * size
            end = begin + size if n < WRITES - 1 else drops
            lax.fori_loop(begin, end, finish, 0, unroll=4)
            send(begin, end - begin)
        for copy in copies:
            copy.wait()
    else:
        lax.fori_loop(0, drops, finish, 0, unroll=4)


VMEM = pl.BlockSpec(memory_space=pltpu.VMEM)
SMEM = pl.BlockSpec(memory_space=pltpu.SMEM)
PARAMS = pltpu.CompilerParams(vmem_limit_bytes=24 * 1024 * 1024)


def cost(flops, bytes_accessed):
    return pl.CostEstimate(flops=flops, bytes_accessed=bytes_accessed, transcendentals=0)


def shift_up(value, axis):
    count = lax.axis_size(axis)
    return lax.ppermute(value, axis, [(i, (i + 1) % count) for i in range(count)])


def shift_down(value, axis):
    count = lax.axis_size(axis)
    return lax.ppermute(value, axis, [((i + 1) % count, i) for i in range(count)])


def shards(
    field,
    courant_x,
    courant_y,
    supersat,
    cloud_mask,
    fall_speed,
    growth,
    activation_threshold,
    kernel_rate,
    partner,
    target,
):
    bins, depth, nx, ny = field.shape
    drops, slots = partner.shape
    f32 = jnp.float32
    blocks = depth // SUB
    flat = field.reshape(bins, depth * nx, ny)
    cx, cy, sat, mask = (
        a.reshape(depth * nx, ny) for a in (courant_x, courant_y, supersat, cloud_mask)
    )

    groups = bins // GROUP
    face = jax.ShapeDtypeStruct((bins, depth, ny), f32)
    to_right, to_left = pl.pallas_call(
        functools.partial(pack_x_kernel, nx),
        out_shape=(face, face),
        in_specs=[VMEM],
        out_specs=(VMEM, VMEM),
        compiler_params=PARAMS,
        cost_estimate=cost(1 << 20, 6 << 20),
        name="pack_x",
    )(flat)
    x_left = shift_up(to_right, "gx")
    x_right = shift_down(to_left, "gx")
    cy, cx_last, to_right, to_left = lax.optimization_barrier((cy, courant_x, to_right, to_left))
    cx_left = shift_up(cx_last[:, nx - 1, :], "gx")

    y_to_right, y_to_left = pl.pallas_call(
        functools.partial(pack_y_kernel, nx),
        out_shape=(
            jax.ShapeDtypeStruct((groups + 1, SUB, LANES), f32),
            jax.ShapeDtypeStruct((groups, SUB, LANES), f32),
        ),
        in_specs=[VMEM, VMEM],
        out_specs=(VMEM, VMEM),
        compiler_params=PARAMS,
        cost_estimate=cost(1 << 22, 1 << 22),
        name="pack_y",
    )(flat, cy)
    y_left = shift_up(y_to_right, "gy")
    y_right = shift_down(y_to_left, "gy")

    ratio = fall_speed / (1.0 + fall_speed)
    log_ratio = jnp.log(ratio)
    sub = jnp.arange(SUB, dtype=f32)
    power = jnp.stack([jnp.full((SUB,), 1.0, f32), jnp.full((SUB,), 2.0, f32), jnp.full((SUB,), 4.0, f32), SUB - sub])
    keep = jnp.stack([sub < SUB - 1, sub < SUB - 2, sub < SUB - 4, sub < SUB])
    table = jnp.where(keep, jnp.exp(log_ratio[:, None, None] * power), 0.0)
    table = jnp.broadcast_to(table[..., None], (bins, 4, SUB, LANES))
    step = jnp.exp(log_ratio[None, :] * (SUB * jnp.arange(blocks - 1, -1, -1, dtype=f32))[:, None])
    scal = jnp.concatenate(
        [
            1.0 / (1.0 + fall_speed),
            step.reshape(-1),
            growth,
            jnp.zeros((1,), f32),
            activation_threshold,
            kernel_rate.reshape(-1),
        ]
    )
    index = jnp.concatenate([partner.reshape(-1), target.reshape(-1)])

    inner_x = tuple(range(1, nx - 1))
    edge_x = (0, nx - 1)

    def settle_shapes(xs):
        return (
            jax.ShapeDtypeStruct((bins, len(xs) * blocks, SUB, LANES), f32),
            jax.ShapeDtypeStruct((len(xs), bins, LANES), f32),
        )

    count = lax.axis_size("gz")
    whole = jnp.exp(log_ratio * depth)[None, :, None]

    def inflow(bottom):
        carry = jnp.zeros_like(bottom)
        for hop in range(count - 1):
            sent = bottom if hop == 0 else bottom + whole * carry
            carry = lax.ppermute(sent, "gz", [(i + 1, i) for i in range(count - 1)])
        return carry

    def micro_part(xs, settled, carry, inner):
        cells = len(xs) * blocks
        args = [scal, index, settled, carry, table, sat, mask] + list(inner)
        if inner:
            out = jax.ShapeDtypeStruct((bins, depth * nx, ny), f32)
        else:
            out = jax.ShapeDtypeStruct((bins, cells, SUB, LANES), f32)
        return pl.pallas_call(
            functools.partial(micro_kernel, nx, xs, slots, bool(inner)),
            out_shape=out,
            in_specs=[SMEM, SMEM] + [VMEM] * (len(args) - 2),
            out_specs=pl.BlockSpec(memory_space=pl.ANY) if inner else VMEM,
            scratch_shapes=[
                pltpu.VMEM((drops, cells, SUB, LANES), f32),
                pltpu.VMEM((drops, cells, SUB, LANES), f32),
            ]
            + ([pltpu.VMEM(out.shape, f32), pltpu.SemaphoreType.DMA((WRITES + 1,))] if inner else []),
            compiler_params=PARAMS,
            cost_estimate=cost(1 << 24, 8 << 20),
            name="micro_edge" if inner else "micro_inner",
        )(*args)

    settled, bottom, part, part_bottom = pl.pallas_call(
        functools.partial(settle_kernel, nx, (inner_x, edge_x)),
        out_shape=settle_shapes(inner_x) + settle_shapes(edge_x),
        in_specs=[SMEM] + [VMEM] * 6,
        out_specs=(VMEM,) * 4,
        compiler_params=PARAMS,
        cost_estimate=cost(1 << 24, 16 << 20),
        name="settle_all",
    )(scal, flat, cx, cy, y_left, y_right, table)
    inner_carry = inflow(bottom)
    edge_settled, edge_bottom = pl.pallas_call(
        functools.partial(edge_kernel, nx),
        out_shape=settle_shapes(edge_x),
        in_specs=[SMEM] + [VMEM] * 8,
        out_specs=(VMEM,) * 2,
        compiler_params=PARAMS,
        cost_estimate=cost(1 << 23, 8 << 20),
        name="settle_edge",
    )(scal, part, part_bottom, cx, table, cx_left, to_left, x_left, x_right)
    settled, edge_bottom = lax.optimization_barrier((settled, edge_bottom))
    edge_carry = inflow(edge_bottom)
    inner = micro_part(inner_x, settled, inner_carry, ())
    out = micro_part(edge_x, edge_settled, edge_carry, (inner,))
    return out.reshape(field.shape)


def solution(mesh):
    cells = P("gz", "gx", "gy")
    return jax.shard_map(
        shards,
        mesh=mesh,
        in_specs=(P(None, "gz", "gx", "gy"), cells, cells, cells, cells) + (P(),) * 6,
        out_specs=P(None, "gz", "gx", "gy"),
        check_vma=False,
    )
```
